128 devices in a mesh: store: 16 (over y, x), req: 4 (over z), tp: 2 (over core).
Axes of the slice: x: 4, y: 4, z: 4, core: 2. Of those that a mesh axis runs over, the one named last changes fastest.
Arguments:
- span_keys: bfloat16 [512, 256, 1024], P('req', 'store', 'tp'), may hold values from -5 to 5
- span_values: bfloat16 [512, 256, 1024], P('req', 'store', 'tp'), may hold values from -5 to 5
- span_row: int32 [512], replicated, may hold values from 0 to 511, as said below
- span_lists: int32 [64, 8], P(('store', 'req')), may hold values from 0 to 511, as said below
- recompute_pos: int32 [64, 128], P(('store', 'req')), may hold values from 0 to 2047, as said below
- fresh_q: bfloat16 [64, 128, 8192], P(('store', 'req'), None, 'tp'), may hold values from -5 to 5
- fresh_k: bfloat16 [64, 128, 1024], P(('store', 'req'), None, 'tp'), may hold values from -5 to 5
- fresh_v: bfloat16 [64, 128, 1024], P(('store', 'req'), None, 'tp'), may hold values from -5 to 5
Outputs:
- attended: bfloat16 [64, 128, 8192], P(('store', 'req'), None, 'tp')
- span_drift: float32 [512], P(('store', 'req', 'tp'))
The draws below stay inside these ranges and needn't reach their ends.
Inputs may be any that keep to these rules, and one draw needn't show every extreme that they name: `span_row`: each span sits in exactly one table row; rows k*128 .. (k+1)*128 - 1 form block k. `span_lists`: A request's 8 spans are distinct; at most 4 of them lie in one block of table rows, and in every draw some request has exactly 4 in one block. `recompute_pos`: entries k*16 .. (k+1)*16 - 1 of a row are distinct ascending positions within k*256 .. (k+1)*256 - 1.
All inputs are finite; a program needn't handle non-finite values.
Results may differ from the reference program's by a relative error of at most 0.0064.
Values may be sent and summed in bfloat16 or wider, within the bound.
No kernel may reach another device: no remote copies, remote signals or barrier semaphores. Data moves between devices by JAX's collectives and lax.ppermute only.
A program may use at most 128 MiB of HBM per device.

```python
import jax
import jax.numpy as jnp
from jax import lax

H = 64
KVH = 8
HD = 128
CPR = 8
CH_SHARD = 128
SPANS = 512
CL = 256
CTX = 2048
RPC = 16
RC = 128
REQUESTS = 64


def span_plan(key):
    perm = jax.random.permutation(jax.random.fold_in(key, 11), SPANS).astype(jnp.int32)
    span_of_row = jnp.zeros((SPANS,), jnp.int32).at[perm].set(jnp.arange(SPANS, dtype=jnp.int32))
    shapes = jnp.array([[0, 0, 0, 0, 1, 1, 1, 1], [0, 0, 1, 1, 2, 2, 3, 3], [0, 0, 0, 0, 1, 1, 2, 3]], jnp.int32)
    blocks = SPANS // CH_SHARD
    kinds = jax.random.randint(jax.random.fold_in(key, 12), (REQUESTS,), 0, 3).astype(jnp.int32).at[0].set(0)
    bases = jax.random.randint(jax.random.fold_in(key, 13), (REQUESTS,), 0, blocks).astype(jnp.int32)
    offsets = shapes[kinds]
    homes = (offsets + bases[:, None]) % blocks
    earlier = jnp.arange(CPR)[:, None] < jnp.arange(CPR)[None, :]
    same = offsets[:, :, None] == offsets[:, None, :]
    ranks = jnp.sum(same & earlier[None], axis=1).astype(jnp.int32)
    raw = jax.random.randint(jax.random.fold_in(key, 14), (REQUESTS, blocks), 0, CH_SHARD).astype(jnp.int32)
    starts = raw * raw // CH_SHARD
    firsts = jnp.take_along_axis(starts, homes, axis=1)
    locals_in = (firsts + ranks) % CH_SHARD
    lists_out = span_of_row[homes * CH_SHARD + locals_in]
    return (perm, lists_out)


def draw_span_row(key, part):
    return span_plan(key)[0]


def draw_span_lists(key, part):
    return span_plan(key)[1]


def draw_recompute_pos(key, part):
    subkeys = jax.random.split(jax.random.fold_in(key, 31), REQUESTS * CPR)
    offsets = jax.vmap(lambda sub: jax.random.permutation(sub, CL)[:RPC])(subkeys)
    offsets = jnp.sort(offsets, axis=1).astype(jnp.int32).reshape(REQUESTS, CPR, RPC)
    places = offsets + (jnp.arange(CPR, dtype=jnp.int32) * CL)[None, :, None]
    return places.reshape(REQUESTS, RC)


def fresh_pair(key):
    keys_new = jax.random.normal(jax.random.fold_in(key, 21), (REQUESTS, RC, KVH * HD), jnp.float32)
    queries = jax.random.normal(jax.random.fold_in(key, 22), (REQUESTS, RC, H * HD), jnp.float32)
    return (jnp.clip(queries, -5.0, 5.0), jnp.clip(keys_new, -5.0, 5.0))


def draw_fresh_q(key, part):
    return fresh_pair(key)[0].astype(jnp.bfloat16)


def draw_fresh_k(key, part):
    return fresh_pair(key)[1].astype(jnp.bfloat16)


def block_scale(rng, extent, shards, least, largest):
    def one(axis_at, blocks):
        heights = jax.random.uniform(jax.random.fold_in(jax.random.fold_in(rng, 6), axis_at), (blocks,), jnp.float32, least / len(shards), largest / len(shards))
        return jnp.repeat(jnp.exp(heights), extent[axis_at] // blocks).reshape((-1,) + (1,) * (len(extent) - axis_at - 1))

    gain = one(*shards[0])
    for cut in shards[1:]:
        gain = gain * one(*cut)
    return gain


def centred(rng, dims, scale, reach, cuts=(), held_as=jnp.bfloat16):
    values = scale * jax.random.normal(rng, dims, jnp.float32)
    if cuts:
        values = values * block_scale(rng, dims, cuts, -0.22, 0.18)
    return jnp.clip(values, -reach, reach).astype(held_as)


def setup_inputs(seed: int = 0) -> dict:
    keys = jax.random.split(jax.random.key(seed), 9)
    span_keys = centred(keys[0], (SPANS, CL, KVH * HD), 1.0, 5.0, ((0, 4), (1, 16), (2, 2)))
    span_values = centred(keys[1], (SPANS, CL, KVH * HD), 1.0, 5.0, ((0, 4), (1, 16), (2, 2)))
    span_row = draw_span_row(jax.random.fold_in(keys[8], 71), 0)
    span_lists = draw_span_lists(jax.random.fold_in(keys[8], 71), 0)
    recompute_pos = draw_recompute_pos(jax.random.fold_in(keys[8], 71), 0)
    fresh_q = draw_fresh_q(jax.random.fold_in(keys[8], 71), 0)
    fresh_k = draw_fresh_k(jax.random.fold_in(keys[8], 71), 0)
    fresh_v = centred(keys[7], (REQUESTS, RC, KVH * HD), 1.0, 5.0, ((0, 64), (2, 2)))
    return {"span_keys": span_keys, "span_values": span_values, "span_row": span_row, "span_lists": span_lists, "recompute_pos": recompute_pos, "fresh_q": fresh_q, "fresh_k": fresh_k, "fresh_v": fresh_v}


def rotate(values, places):
    half = HD // 2
    freq = jnp.exp(-jnp.log(500000.0) * jnp.arange(half, dtype=jnp.float32) / half)
    angles = places.astype(jnp.float32)[:, None] * freq[None, :]
    cosine = jnp.cos(angles)[:, None, :]
    sine = jnp.sin(angles)[:, None, :]
    first = values[..., :half]
    second = values[..., half:]
    return jnp.concatenate([first * cosine - second * sine, second * cosine + first * sine], axis=-1)


def reference(span_keys, span_values, span_row, span_lists, recompute_pos, fresh_q, fresh_k, fresh_v):
    features = KVH * HD
    group_size = H // KVH
    scale = HD ** -0.5
    positions = jnp.arange(CTX, dtype=jnp.int32)

    def one_request(members):
        listed, places, queries_in, keys_in, values_in = members
        table_rows = span_row[listed]
        keys_raw = span_keys[table_rows].reshape(CTX, features)
        values_raw = span_values[table_rows].reshape(CTX, features)
        keys_rot = rotate(keys_raw.astype(jnp.float32).reshape(CTX, KVH, HD), positions).astype(jnp.bfloat16).reshape(CTX, features)
        new_keys = rotate(keys_in.astype(jnp.float32).reshape(RC, KVH, HD), places).astype(jnp.bfloat16).reshape(RC, features)
        keys_all = keys_rot.at[places].set(new_keys)
        values_all = values_raw.at[places].set(values_in)
        queries = rotate(queries_in.astype(jnp.float32).reshape(RC, H, HD), places).astype(jnp.bfloat16)
        visible = positions[None, :] <= places[:, None]
        query_heads = queries.reshape(RC, KVH, group_size, HD).transpose(1, 2, 0, 3)
        key_heads = keys_all.reshape(CTX, KVH, HD).transpose(1, 0, 2)
        value_heads = values_all.reshape(CTX, KVH, HD).transpose(1, 0, 2)

        def one_head(parts):
            query_block, key_block, value_block = parts
            scores = jnp.einsum("hqd,kd->hqk", query_block.astype(jnp.float32), key_block.astype(jnp.float32)) * scale
            scores = jnp.where(visible[None], scores, -1e30)
            row_max = jnp.max(scores, axis=-1, keepdims=True)
            weights = jnp.exp(scores - row_max)
            probabilities = (weights / jnp.sum(weights, axis=-1, keepdims=True)).astype(jnp.bfloat16)
            return jnp.einsum("hqk,kd->hqd", probabilities.astype(jnp.float32), value_block.astype(jnp.float32)).astype(jnp.bfloat16)

        result = lax.map(one_head, (query_heads, key_heads, value_heads))
        result = result.transpose(2, 0, 1, 3).reshape(RC, H * HD)
        cached_k = keys_raw[places].astype(jnp.float32)
        cached_v = values_raw[places].astype(jnp.float32)
        deviation = jnp.sum((keys_in.astype(jnp.float32) - cached_k) ** 2 + (values_in.astype(jnp.float32) - cached_v) ** 2, axis=1) / (2.0 * features)
        span_share = jnp.mean(deviation.reshape(CPR, RPC), axis=1)
        return result, span_share

    attended, shares = lax.map(one_request, (span_lists, recompute_pos, fresh_q, fresh_k, fresh_v))
    drift_total = jnp.zeros((SPANS,), jnp.float32).at[span_lists.reshape(-1)].add(shares.reshape(-1))
    return attended, drift_total
```

```python
import functools

import jax
import jax.numpy as jnp
import numpy as np
from jax import lax
from jax.experimental import pallas as pl
from jax.experimental.pallas import tpu as pltpu
from jax.sharding import PartitionSpec as P

HD = 128
HALF = HD // 2
CPR = 8
RPC = 16
CL = 256
CTX = CPR * CL
RC = CPR * RPC
KVH = 8
CAP = 4
LANES = 128
SCALE_LOG2E = float(HD ** -0.5 * np.log2(np.e))

FREQ = np.exp(-np.log(500000.0) * np.arange(HALF) / HALF).astype(np.float32)


def context_tables():
    angles = (np.arange(CTX, dtype=np.float32)[:, None] * FREQ[None, :]).astype(np.float64)
    cosine = np.cos(angles).astype(np.float32)
    sine = np.sin(angles).astype(np.float32)
    return (
        np.concatenate([cosine, cosine], axis=1),
        np.concatenate([-sine, sine], axis=1),
    )


COS_CTX, SIN_CTX = context_tables()


def turn(x, cosine, sine):
    return x * cosine + pltpu.roll(x, HALF, 1) * sine


def span_homes(span_row, span_lists, shard_rows):
    rows = [span_row[span_lists[0, j]] for j in range(CPR)]
    homes = [row // shard_rows for row in rows]
    slots = [row % shard_rows for row in rows]
    ranks = []
    for j in range(CPR):
        rank = jnp.int32(0)
        for i in range(j):
            rank = rank + jnp.where(homes[i] == homes[j], 1, 0)
        ranks.append(rank)
    return homes, slots, ranks


def ask_kernel(shard_rows, blocks, span_row, span_lists, out):
    homes, slots, ranks = span_homes(span_row, span_lists, shard_rows)
    block = lax.broadcasted_iota(jnp.int32, out.shape, 0) % blocks
    lane = lax.broadcasted_iota(jnp.int32, out.shape, 1)
    total = jnp.zeros(out.shape, jnp.int32)
    for j in range(CPR):
        total = jnp.where((block == homes[j]) & (lane == ranks[j]), slots[j], total)
    out[...] = total


def pick_kernel(wanted, keys, values, send, sem):
    def body(r, carry):
        for t in range(CAP):
            row = wanted[r, t]
            pltpu.make_async_copy(keys.at[row], send.at[r, t, 0], sem).start()
            pltpu.make_async_copy(values.at[row], send.at[r, t, 1], sem).start()
        return carry

    lax.fori_loop(0, send.shape[0], body, 0)
    pltpu.make_async_copy(send, send, sem).wait()


def fresh_kernel(heads_kv, group, q, k, cosine, sine, q_out, k_out):
    cos = cosine[...]
    sin = sine[...]
    for h in range(heads_kv):
        cols = slice(h * HD, (h + 1) * HD)
        k_out[:, cols] = turn(k[:, cols].astype(jnp.float32), cos, sin).astype(jnp.bfloat16)
        for g in range(group):
            n = h * group + g
            turned = turn(q[:, n * HD : (n + 1) * HD].astype(jnp.float32), cos, sin)
            turned = turned.astype(jnp.bfloat16)
            for j in range(CPR):
                q_out[h * CPR + j, g * RPC : (g + 1) * RPC, :] = turned[j * RPC : (j + 1) * RPC]


def fetch(got, homes, ranks, which, buf, sems):
    copies = []
    for j in range(CPR):
        copies.append(
            pltpu.make_async_copy(got.at[:, homes[j], ranks[j], which], buf.at[j], sems.at[which, j])
        )
    return copies


def drift_kernel(
    shard_rows, span_row, span_lists, places, fresh_k, fresh_v, got, out, kbuf, vbuf, sems
):
    homes, _, ranks = span_homes(span_row, span_lists, shard_rows)
    width = fresh_k.shape[1]
    key_copies = fetch(got, homes, ranks, 0, kbuf, sems)
    value_copies = fetch(got, homes, ranks, 1, vbuf, sems)
    for j in range(CPR):
        key_copies[j].start()
        value_copies[j].start()
    dest = lax.broadcasted_iota(jnp.int32, out.shape, 0)
    lane = lax.broadcasted_iota(jnp.int32, out.shape, 1)
    per_dest = (span_row.shape[0]) // out.shape[0]
    total = jnp.zeros(out.shape, jnp.float32)
    token = lax.broadcasted_iota(jnp.int32, (RPC, CL), 1)
    for j in range(CPR):
        rows = slice(j * RPC, (j + 1) * RPC)
        pick = (token + j * CL == places[rows, :]).astype(jnp.float32).astype(jnp.bfloat16)
        gap = jnp.zeros((RPC, width), jnp.float32)
        for copy, buf, fresh in (
            (key_copies[j], kbuf, fresh_k),
            (value_copies[j], vbuf, fresh_v),
        ):
            copy.wait()
            cached = jnp.dot(
                pick, buf[j].reshape(CL, width), preferred_element_type=jnp.float32
            )
            delta = fresh[rows, :].astype(jnp.float32) - cached
            gap = gap + delta * delta
        share = jnp.sum(gap) * (1.0 / (2.0 * KVH * HD * RPC))
        span = span_lists[0, j]
        total = total + jnp.where(
            (dest == span // per_dest) & (lane == span % per_dest), share, 0.0
        )
    out[...] = total


def attend_kernel(
    shard_rows,
    heads_kv,
    group,
    span_row,
    span_lists,
    places_row,
    places_col,
    q,
    new_k,
    new_v,
    cosine,
    sine,
    got,
    out,
    kbuf,
    vbuf,
    keys,
    vals,
    seen,
    sems,
):
    homes, _, ranks = span_homes(span_row, span_lists, shard_rows)
    key_copies = fetch(got, homes, ranks, 0, kbuf, sems)
    value_copies = fetch(got, homes, ranks, 1, vbuf, sems)
    for j in range(CPR):
        key_copies[j].start()
        value_copies[j].start()
    token_row = lax.broadcasted_iota(jnp.int32, (CL, RPC), 0)
    token_lane = lax.broadcasted_iota(jnp.int32, (RPC, CL), 1)
    ones = jnp.ones((RPC, HD), jnp.bfloat16)
    for j in range(CPR):
        rows = slice(j * RPC, (j + 1) * RPC)
        span = slice(j * CL, (j + 1) * CL)
        seen[j] = jnp.where(token_lane + j * CL <= places_col[rows, :], 0.0, -1e30)
        put = (token_row + j * CL == places_row[j : j + 1, :]).astype(jnp.float32)
        put = put.astype(jnp.bfloat16)
        replaced = jnp.dot(put, ones, preferred_element_type=jnp.float32) > 0.5
        cos = cosine[span, :]
        sin = sine[span, :]
        key_copies[j].wait()
        value_copies[j].wait()
        for h in range(heads_kv):
            cols = slice(h * HD, (h + 1) * HD)
            raw = kbuf[j, :, :, cols].reshape(CL, HD).astype(jnp.float32)
            fresh = jnp.dot(put, new_k[rows, cols], preferred_element_type=jnp.float32)
            keys[h, span, :] = jnp.where(replaced, fresh, turn(raw, cos, sin)).astype(jnp.bfloat16)
            raw = vbuf[j, :, :, cols].reshape(CL, HD).astype(jnp.float32)
            fresh = jnp.dot(put, new_v[rows, cols], preferred_element_type=jnp.float32)
            vals[h, span, :] = jnp.where(replaced, fresh, raw).astype(jnp.bfloat16)

    def head(h, carry):
        for j in range(CPR):
            extent = (j + 1) * CL
            scores = lax.dot_general(
                q[h * CPR + j],
                keys[h, :extent, :],
                (((1,), (1,)), ((), ())),
                preferred_element_type=jnp.float32,
            )
            bias = jnp.concatenate([seen[j]] * group, axis=0)
            last = scores[:, j * CL :] + bias
            scores = last if j == 0 else jnp.concatenate([scores[:, : j * CL], last], axis=1)
            row_max = jnp.max(scores, axis=1, keepdims=True)
            weights = jnp.exp2((scores - row_max) * SCALE_LOG2E)
            row_sum = jnp.sum(weights, axis=1, keepdims=True)
            mixed = jnp.dot(
                weights.astype(jnp.bfloat16),
                vals[h, :extent, :],
                preferred_element_type=jnp.float32,
            )
            mixed = (mixed / row_sum).astype(jnp.bfloat16)
            for g in range(group):
                start = pl.multiple_of((h * group + g) * HD, HD)
                out[j * RPC : (j + 1) * RPC, pl.ds(start, HD)] = mixed[g * RPC : (g + 1) * RPC]
        return carry

    lax.fori_loop(0, heads_kv, head, 0)


SMEM = pl.BlockSpec(memory_space=pltpu.SMEM)
VMEM = pl.BlockSpec(memory_space=pltpu.VMEM)
ANY = pl.BlockSpec(memory_space=pl.ANY)


def local(span_keys, span_values, span_row, span_lists, recompute_pos, fresh_q, fresh_k, fresh_v):
    n_store = lax.axis_size("store")
    n_req = lax.axis_size("req")
    n_tp = lax.axis_size("tp")
    n_all = n_store * n_req * n_tp
    peers = n_store * n_req
    shard_rows, tok_dev, width = span_keys.shape
    heads_kv = width // HD
    heads_q = fresh_q.shape[2] // HD
    group = heads_q // heads_kv
    bf16 = jnp.bfloat16
    params = functools.partial(pltpu.CompilerParams, vmem_limit_bytes=48 << 20)

    ask = pl.pallas_call(
        functools.partial(ask_kernel, shard_rows, n_req),
        out_shape=jax.ShapeDtypeStruct((peers, LANES), jnp.int32),
        in_specs=[SMEM, SMEM],
        out_specs=VMEM,
        name="ask",
    )(span_row, span_lists)
    wanted = lax.all_to_all(ask, ("store", "req"), split_axis=0, concat_axis=0, tiled=True)

    send = pl.pallas_call(
        pick_kernel,
        out_shape=jax.ShapeDtypeStruct((peers, CAP, 2, tok_dev, width), bf16),
        in_specs=[SMEM, ANY, ANY],
        out_specs=ANY,
        scratch_shapes=[pltpu.SemaphoreType.DMA],
        name="pick",
    )(wanted, span_keys, span_values)
    got = lax.all_to_all(send, ("store", "req"), split_axis=0, concat_axis=0, tiled=True)
    got = got.reshape(n_store, n_req, CAP, 2, tok_dev, width)

    places, raw_q, raw_k, _ = lax.optimization_barrier((recompute_pos, fresh_q, fresh_k, send))
    places = places[0]
    raw_k = raw_k[0]
    new_v = fresh_v[0]
    angles = places.astype(jnp.float32)[:, None] * jnp.asarray(FREQ)[None, :]
    cosine = jnp.cos(angles)
    sine = jnp.sin(angles)
    queries, new_k = pl.pallas_call(
        functools.partial(fresh_kernel, heads_kv, group),
        out_shape=(
            jax.ShapeDtypeStruct((heads_kv * CPR, group * RPC, HD), bf16),
            jax.ShapeDtypeStruct((RC, width), bf16),
        ),
        in_specs=[VMEM] * 4,
        out_specs=(VMEM, VMEM),
        compiler_params=params(),
        name="fresh",
    )(
        raw_q[0],
        raw_k,
        jnp.concatenate([cosine, cosine], axis=1),
        jnp.concatenate([-sine, sine], axis=1),
    )
    places_col = places[:, None]
    places_row = places.reshape(CPR, RPC)

    part = pl.pallas_call(
        functools.partial(drift_kernel, shard_rows),
        out_shape=jax.ShapeDtypeStruct((n_all, LANES), jnp.float32),
        in_specs=[SMEM, SMEM, VMEM, VMEM, VMEM, ANY],
        out_specs=VMEM,
        scratch_shapes=[
            pltpu.VMEM((CPR, n_store, tok_dev, width), bf16),
            pltpu.VMEM((CPR, n_store, tok_dev, width), bf16),
            pltpu.SemaphoreType.DMA((2, CPR)),
        ],
        compiler_params=params(),
        cost_estimate=pl.CostEstimate(
            flops=4 * RC * CTX * width // CPR, bytes_accessed=4 * CTX * width, transcendentals=0
        ),
        name="drift",
    )(span_row, span_lists, places_col, raw_k, new_v, got)
    parts = lax.all_to_all(part, ("store", "req", "tp"), split_axis=0, concat_axis=0, tiled=True)

    attended = pl.pallas_call(
        functools.partial(attend_kernel, shard_rows, heads_kv, group),
        out_shape=jax.ShapeDtypeStruct((RC, heads_q * HD), bf16),
        in_specs=[SMEM, SMEM] + [VMEM] * 7 + [ANY],
        out_specs=VMEM,
        scratch_shapes=[
            pltpu.VMEM((CPR, n_store, tok_dev, width), bf16),
            pltpu.VMEM((CPR, n_store, tok_dev, width), bf16),
            pltpu.VMEM((heads_kv, CTX, HD), bf16),
            pltpu.VMEM((heads_kv, CTX, HD), bf16),
            pltpu.VMEM((CPR, RPC, CL), jnp.float32),
            pltpu.SemaphoreType.DMA((2, CPR)),
        ],
        compiler_params=params(),
        cost_estimate=pl.CostEstimate(
            flops=2 * heads_q * RC * CTX * HD * 2,
            bytes_accessed=4 * CTX * width + 4 * RC * heads_q * HD,
            transcendentals=heads_q * RC * CTX // 2,
        ),
        name="attend",
    )(
        span_row,
        span_lists,
        places_row,
        places_col,
        queries,
        new_k,
        new_v,
        jnp.asarray(COS_CTX),
        jnp.asarray(SIN_CTX),
        got,
    )
    per_dest = span_row.shape[0] // n_all
    drift_part = jnp.sum(parts, axis=0)[:per_dest]
    return (attended[None], drift_part)


def solution(mesh):
    in_specs = (
        P("req", "store", "tp"),
        P("req", "store", "tp"),
        P(),
        P(("store", "req"), None),
        P(("store", "req"), None),
        P(("store", "req"), None, "tp"),
        P(("store", "req"), None, "tp"),
        P(("store", "req"), None, "tp"),
    )
    out_specs = (P(("store", "req"), None, "tp"), P(("store", "req", "tp")))
    return jax.shard_map(local, mesh=mesh, in_specs=in_specs, out_specs=out_specs, check_vma=False)
```

```python
import functools

import jax
import jax.numpy as jnp
import numpy as np
from jax import lax
from jax.experimental import pallas as pl
from jax.experimental.pallas import tpu as pltpu
from jax.sharding import PartitionSpec as P

HD = 128
HALF = HD // 2
CPR = 8
RPC = 16
CL = 256
CTX = CPR * CL
RC = CPR * RPC
KVH = 8
CAP = 4
LANES = 128
SCALE_LOG2E = float(HD ** -0.5 * np.log2(np.e))

FREQ = np.exp(-np.log(500000.0) * np.arange(HALF) / HALF).astype(np.float32)


def angle_tables(positions):
    angles = positions[:, None].astype(np.float64) * FREQ[None, :].astype(np.float64)
    cosine = np.cos(angles).astype(np.float32)
    sine = np.sin(angles).astype(np.float32)
    return (
        np.concatenate([cosine, cosine], axis=1),
        np.concatenate([-sine, sine], axis=1),
    )


COS_SPAN, SIN_SPAN = angle_tables(CL * np.arange(CPR))
COS_TOKEN, SIN_TOKEN = angle_tables(np.arange(CL))


def turn(x, cosine, sine):
    return x * cosine + pltpu.roll(x, HALF, 1) * sine


def span_homes(span_row, span_lists, shard_rows):
    rows = [span_row[span_lists[0, j]] for j in range(CPR)]
    homes = [row // shard_rows for row in rows]
    slots = [row % shard_rows for row in rows]
    ranks = []
    for j in range(CPR):
        rank = jnp.int32(0)
        for i in range(j):
            rank = rank + jnp.where(homes[i] == homes[j], 1, 0)
        ranks.append(rank)
    return homes, slots, ranks


def ask_kernel(shard_rows, blocks, span_row, span_lists, out):
    homes, slots, ranks = span_homes(span_row, span_lists, shard_rows)
    block = lax.broadcasted_iota(jnp.int32, out.shape, 0) % blocks
    lane = lax.broadcasted_iota(jnp.int32, out.shape, 1)
    total = jnp.zeros(out.shape, jnp.int32)
    for j in range(CPR):
        total = jnp.where((block == homes[j]) & (lane == ranks[j]), slots[j], total)
    out[...] = total


def pick_kernel(wanted, keys, values, send, key_rows, value_rows, stage, in_sems, out_sem):
    loads = [
        pltpu.make_async_copy(table, rows, in_sems.at[i])
        for i, (table, rows) in enumerate(((keys, key_rows), (values, value_rows)))
    ]
    for load in loads:
        load.start()
    for load in loads:
        load.wait()

    def fill(r, carry):
        for t in range(CAP):
            row = wanted[r, t]
            stage[r, t, 0] = key_rows[row]
            stage[r, t, 1] = value_rows[row]
        pltpu.make_async_copy(stage.at[r], send.at[r], out_sem).start()
        return carry

    lax.fori_loop(0, send.shape[0], fill, 0, unroll=4)
    pltpu.make_async_copy(stage, send, out_sem).wait()


def fresh_kernel(heads_kv, group, q, k, cosine, sine, q_out, k_out):
    cos = cosine[...]
    sin = sine[...]
    for h in range(heads_kv):
        cols = slice(h * HD, (h + 1) * HD)
        k_out[:, cols] = turn(k[:, cols].astype(jnp.float32), cos, sin).astype(jnp.bfloat16)
        for g in range(group):
            n = h * group + g
            turned = turn(q[:, n * HD : (n + 1) * HD].astype(jnp.float32), cos, sin)
            turned = turned.astype(jnp.bfloat16)
            for j in range(CPR):
                q_out[h * CPR + j, g * RPC : (g + 1) * RPC, :] = turned[j * RPC : (j + 1) * RPC]


def prepare_kernel(
    shard_rows,
    heads_kv,
    span_row,
    span_lists,
    places_row,
    places_col,
    fresh_k,
    fresh_v,
    new_k,
    cos_span,
    sin_span,
    cos_token,
    sin_token,
    got,
    keys,
    vals,
    drift,
    kbuf,
    vbuf,
    key_stage,
    value_stage,
    sems,
    out_sem,
):
    homes, _, ranks = span_homes(span_row, span_lists, shard_rows)
    copies = []
    for j in range(CPR):
        pair = [
            pltpu.make_async_copy(got.at[:, homes[j], ranks[j], which], buf.at[j], sems.at[which, j])
            for which, buf in enumerate((kbuf, vbuf))
        ]
        for copy in pair:
            copy.start()
        copies.append(pair)
    width = fresh_k.shape[1]
    dest = lax.broadcasted_iota(jnp.int32, drift.shape, 0)
    lane = lax.broadcasted_iota(jnp.int32, drift.shape, 1)
    per_dest = span_row.shape[0] // drift.shape[0]
    total = jnp.zeros(drift.shape, jnp.float32)
    token_row = lax.broadcasted_iota(jnp.int32, (CL, RPC), 0)
    token_lane = lax.broadcasted_iota(jnp.int32, (RPC, CL), 1)
    ones = jnp.ones((RPC, HD), jnp.bfloat16)
    stores = []
    for j in range(CPR):
        rows = slice(j * RPC, (j + 1) * RPC)
        span = slice(j * CL, (j + 1) * CL)
        take = (token_lane + j * CL == places_col[rows, :]).astype(jnp.float32)
        take = take.astype(jnp.bfloat16)
        put = (token_row + j * CL == places_row[j : j + 1, :]).astype(jnp.float32)
        put = put.astype(jnp.bfloat16)
        replaced = jnp.dot(put, ones, preferred_element_type=jnp.float32) > 0.5
        ca, sa = cos_span[j : j + 1, :], sin_span[j : j + 1, :]
        cb, sb = cos_token[...], sin_token[...]
        cos = ca * cb - sa * sb
        sin = sa * cb + ca * sb
        gap = jnp.zeros((RPC, width), jnp.float32)
        for copy, buf, fresh in zip(copies[j], (kbuf, vbuf), (fresh_k, fresh_v)):
            copy.wait()
            cached = jnp.dot(take, buf[j].reshape(CL, width), preferred_element_type=jnp.float32)
            delta = fresh[rows, :].astype(jnp.float32) - cached
            gap = gap + delta * delta
        share = jnp.sum(gap) * (1.0 / (2.0 * KVH * HD * RPC))
        chosen = span_lists[0, j]
        total = total + jnp.where(
            (dest == chosen // per_dest) & (lane == chosen % per_dest), share, 0.0
        )
        for h in range(heads_kv):
            cols = slice(h * HD, (h + 1) * HD)
            raw = kbuf[j, :, :, cols].reshape(CL, HD).astype(jnp.float32)
            new = jnp.dot(put, new_k[rows, cols], preferred_element_type=jnp.float32)
            ready = jnp.where(replaced, new, turn(raw, cos, sin))
            key_stage[j, h] = ready.astype(jnp.bfloat16)
            raw = vbuf[j, :, :, cols].reshape(CL, HD).astype(jnp.float32)
            new = jnp.dot(put, fresh_v[rows, cols], preferred_element_type=jnp.float32)
            value_stage[j, h] = jnp.where(replaced, new, raw).astype(jnp.bfloat16)
        for stage, whole in ((key_stage, keys), (value_stage, vals)):
            copy = pltpu.make_async_copy(stage.at[j], whole.at[:, span], out_sem)
            copy.start()
            stores.append(copy)
    drift[...] = total
    for copy in stores:
        copy.wait()


def attend_kernel(
    heads_kv, group, places_col, q, all_keys, all_vals, out, keys, vals, seen, scores, sems
):
    pairs = ((all_keys, keys), (all_vals, vals))
    for h in range(heads_kv):
        for which, (whole, buf) in enumerate(pairs):
            pltpu.make_async_copy(whole.at[h], buf.at[h], sems.at[which, h]).start()
    block = group * RPC
    token = lax.broadcasted_iota(jnp.int32, (RPC, CL), 1)
    for j in range(CPR):
        rows = slice(j * RPC, (j + 1) * RPC)
        seen[j] = jnp.where(token + j * CL <= places_col[rows, :], 0.0, -1e30)

    def head(h, carry):
        for which, (whole, buf) in enumerate(pairs):
            pltpu.make_async_copy(whole.at[h], buf.at[h], sems.at[which, h]).wait()
        for t in range(CPR):
            later = q[pl.ds(h * CPR + t, CPR - t)].reshape((CPR - t) * block, HD)
            scores[t * block :, t * CL : (t + 1) * CL] = lax.dot_general(
                later,
                keys[h, t * CL : (t + 1) * CL, :],
                (((1,), (1,)), ((), ())),
                preferred_element_type=jnp.float32,
            )
        for j in range(CPR):
            extent = (j + 1) * CL
            part = scores[j * block : (j + 1) * block, :extent]
            bias = jnp.concatenate([seen[j]] * group, axis=0)
            last = part[:, j * CL :] + bias
            part = last if j == 0 else jnp.concatenate([part[:, : j * CL], last], axis=1)
            row_max = jnp.max(part, axis=1, keepdims=True)
            weights = jnp.exp2((part - row_max) * SCALE_LOG2E)
            row_sum = jnp.sum(weights, axis=1, keepdims=True)
            mixed = jnp.dot(
                weights.astype(jnp.bfloat16),
                vals[h, :extent, :],
                preferred_element_type=jnp.float32,
            )
            mixed = (mixed / row_sum).astype(jnp.bfloat16)
            for g in range(group):
                start = pl.multiple_of((h * group + g) * HD, HD)
                out[j * RPC : (j + 1) * RPC, pl.ds(start, HD)] = mixed[g * RPC : (g + 1) * RPC]
        return carry

    lax.fori_loop(0, heads_kv, head, 0)


SMEM = pl.BlockSpec(memory_space=pltpu.SMEM)
VMEM = pl.BlockSpec(memory_space=pltpu.VMEM)
ANY = pl.BlockSpec(memory_space=pl.ANY)


def local(span_keys, span_values, span_row, span_lists, recompute_pos, fresh_q, fresh_k, fresh_v):
    n_store = lax.axis_size("store")
    n_req = lax.axis_size("req")
    n_tp = lax.axis_size("tp")
    n_all = n_store * n_req * n_tp
    peers = n_store * n_req
    shard_rows, tok_dev, width = span_keys.shape
    heads_kv = width // HD
    heads_q = fresh_q.shape[2] // HD
    group = heads_q // heads_kv
    bf16 = jnp.bfloat16

    def params(mebibytes):
        return pltpu.CompilerParams(vmem_limit_bytes=mebibytes << 20)


    ask = pl.pallas_call(
        functools.partial(ask_kernel, shard_rows, n_req),
        out_shape=jax.ShapeDtypeStruct((peers, LANES), jnp.int32),
        in_specs=[SMEM, SMEM],
        out_specs=VMEM,
        name="ask",
    )(span_row, span_lists)
    wanted = lax.all_to_all(ask, ("store", "req"), split_axis=0, concat_axis=0, tiled=True)

    send = pl.pallas_call(
        pick_kernel,
        out_shape=jax.ShapeDtypeStruct((peers, CAP, 2, tok_dev, width), bf16),
        in_specs=[SMEM, ANY, ANY],
        out_specs=ANY,
        scratch_shapes=[
            pltpu.VMEM((shard_rows, tok_dev, width), bf16),
            pltpu.VMEM((shard_rows, tok_dev, width), bf16),
            pltpu.VMEM((peers, CAP, 2, tok_dev, width), bf16),
            pltpu.SemaphoreType.DMA((2,)),
            pltpu.SemaphoreType.DMA,
        ],
        compiler_params=params(58),
        name="pick",
    )(wanted, span_keys, span_values)
    got = lax.all_to_all(send, ("store", "req"), split_axis=0, concat_axis=0, tiled=True)
    got = got.reshape(n_store, n_req, CAP, 2, tok_dev, width)

    places, raw_q, raw_k, _ = lax.optimization_barrier((recompute_pos, fresh_q, fresh_k, send))
    places = places[0]
    raw_k = raw_k[0]
    new_v = fresh_v[0]
    angles = places.astype(jnp.float32)[:, None] * jnp.asarray(FREQ)[None, :]
    cosine = jnp.cos(angles)
    sine = jnp.sin(angles)
    queries, new_k = pl.pallas_call(
        functools.partial(fresh_kernel, heads_kv, group),
        out_shape=(
            jax.ShapeDtypeStruct((heads_kv * CPR, group * RPC, HD), bf16),
            jax.ShapeDtypeStruct((RC, width), bf16),
        ),
        in_specs=[VMEM] * 4,
        out_specs=(VMEM, VMEM),
        compiler_params=params(16),
        name="fresh",
    )(
        raw_q[0],
        raw_k,
        jnp.concatenate([cosine, cosine], axis=1),
        jnp.concatenate([-sine, sine], axis=1),
    )
    places_col = places[:, None]
    places_row = places.reshape(CPR, RPC)

    keys, vals, part = pl.pallas_call(
        functools.partial(prepare_kernel, shard_rows, heads_kv),
        out_shape=(
            jax.ShapeDtypeStruct((heads_kv, CTX, HD), bf16),
            jax.ShapeDtypeStruct((heads_kv, CTX, HD), bf16),
            jax.ShapeDtypeStruct((n_all, LANES), jnp.float32),
        ),
        in_specs=[SMEM, SMEM] + [VMEM] * 9 + [ANY],
        out_specs=(ANY, ANY, VMEM),
        scratch_shapes=[
            pltpu.VMEM((CPR, n_store, tok_dev, width), bf16),
            pltpu.VMEM((CPR, n_store, tok_dev, width), bf16),
            pltpu.VMEM((CPR, heads_kv, CL, HD), bf16),
            pltpu.VMEM((CPR, heads_kv, CL, HD), bf16),
            pltpu.SemaphoreType.DMA((2, CPR)),
            pltpu.SemaphoreType.DMA,
        ],
        compiler_params=params(52),
        cost_estimate=pl.CostEstimate(
            flops=8 * RC * CTX * width // CPR, bytes_accessed=8 * CTX * width, transcendentals=0
        ),
        name="prepare",
    )(
        span_row,
        span_lists,
        places_row,
        places_col,
        raw_k,
        new_v,
        new_k,
        jnp.asarray(COS_SPAN),
        jnp.asarray(SIN_SPAN),
        jnp.asarray(COS_TOKEN),
        jnp.asarray(SIN_TOKEN),
        got,
    )
    parts = lax.all_to_all(part, ("store", "req", "tp"), split_axis=0, concat_axis=0, tiled=True)

    attended = pl.pallas_call(
        functools.partial(attend_kernel, heads_kv, group),
        out_shape=jax.ShapeDtypeStruct((RC, heads_q * HD), bf16),
        in_specs=[VMEM, VMEM, ANY, ANY],
        out_specs=VMEM,
        scratch_shapes=[
            pltpu.VMEM((heads_kv, CTX, HD), bf16),
            pltpu.VMEM((heads_kv, CTX, HD), bf16),
            pltpu.VMEM((CPR, RPC, CL), jnp.float32),
            pltpu.VMEM((CPR * group * RPC, CTX), jnp.float32),
            pltpu.SemaphoreType.DMA((2, heads_kv)),
        ],
        compiler_params=params(59),
        cost_estimate=pl.CostEstimate(
            flops=2 * heads_q * RC * CTX * HD * 2,
            bytes_accessed=4 * CTX * width + 4 * RC * heads_q * HD,
            transcendentals=heads_q * RC * CTX // 2,
        ),
        name="attend",
    )(places_col, queries, keys, vals)
    per_dest = span_row.shape[0] // n_all
    drift_part = jnp.sum(parts, axis=0)[:per_dest]
    return (attended[None], drift_part)


def solution(mesh):
    in_specs = (
        P("req", "store", "tp"),
        P("req", "store", "tp"),
        P(),
        P(("store", "req"), None),
        P(("store", "req"), None),
        P(("store", "req"), None, "tp"),
        P(("store", "req"), None, "tp"),
        P(("store", "req"), None, "tp"),
    )
    out_specs = (P(("store", "req"), None, "tp"), P(("store", "req", "tp")))
    return jax.shard_map(local, mesh=mesh, in_specs=in_specs, out_specs=out_specs, check_vma=False)
```

```python
import functools

import jax
import jax.numpy as jnp
import numpy as np
from jax import lax
from jax.experimental import pallas as pl
from jax.experimental.pallas import tpu as pltpu
from jax.sharding import PartitionSpec as P

HD = 128
HALF = HD // 2
CPR = 8
RPC = 16
CL = 256
CTX = CPR * CL
RC = CPR * RPC
KVH = 8
BLOCKS = 4
SLOTS = CPR // BLOCKS
SIZES = (24, 32, 40)
KEPT, UP, DOWN, FROM_BELOW, FROM_ABOVE, LOADS = 0, 4, 8, 12, 13, 16
LANES = 128
SCALE_LOG2E = float(HD ** -0.5 * np.log2(np.e))

FREQ = np.exp(-np.log(500000.0) * np.arange(HALF) / HALF).astype(np.float32)


def angle_tables(positions):
    angles = positions[:, None].astype(np.float64) * FREQ[None, :].astype(np.float64)
    cosine = np.cos(angles).astype(np.float32)
    sine = np.sin(angles).astype(np.float32)
    return (
        np.concatenate([cosine, cosine], axis=1),
        np.concatenate([-sine, sine], axis=1),
    )


COS_SPAN, SIN_SPAN = angle_tables(CL * np.arange(CPR))
COS_TOKEN, SIN_TOKEN = angle_tables(np.arange(CL))


def turn(x, cosine, sine):
    return x * cosine + pltpu.roll(x, HALF, 1) * sine


def ask_kernel(shard_rows, span_row, span_lists, plan, place):
    spans = [span_row[span_lists[0, j]] for j in range(CPR)]
    homes = [row // shard_rows for row in spans]
    rows = [row % shard_rows for row in spans]
    one = [[jnp.where(home == k, 1, 0) for home in homes] for k in range(BLOCKS)]
    counts = [sum(one[k]) for k in range(BLOCKS)]
    sums = []
    total = jnp.int32(0)
    for k in range(BLOCKS):
        total = total + counts[k] - SLOTS
        sums.append(total)
    low, high = jnp.minimum(sums[0], sums[1]), jnp.maximum(sums[0], sums[1])
    low2, high2 = jnp.minimum(sums[2], sums[3]), jnp.maximum(sums[2], sums[3])
    middle, middle2 = jnp.maximum(low, low2), jnp.minimum(high, high2)
    odd = lax.rem(span_lists[0, 0], 2) == 1
    shift = jnp.where(odd, jnp.maximum(middle, middle2), jnp.minimum(middle, middle2))
    flow = [x - shift for x in sums]
    up = [jnp.maximum(x, 0) for x in flow]
    down = [jnp.maximum(-flow[k - 1], 0) for k in range(BLOCKS)]
    keep = [counts[k] - up[k] - down[k] for k in range(BLOCKS)]

    block = lax.broadcasted_iota(jnp.int32, plan.shape, 0) % BLOCKS
    lane = lax.broadcasted_iota(jnp.int32, plan.shape, 1)
    out = jnp.zeros(plan.shape, jnp.int32)
    for k in range(BLOCKS):
        own = block == k
        heads = (
            (KEPT, keep[k]),
            (UP, up[k]),
            (DOWN, down[k]),
            (FROM_BELOW, up[k - 1]),
            (FROM_ABOVE, down[(k + 1) % BLOCKS]),
        )
        for at, value in heads:
            out = jnp.where(own & (lane == at), value, out)
        out = jnp.where(lane == LOADS + k, up[k], out)
        out = jnp.where(lane == LOADS + BLOCKS + k, down[k], out)

    def of(table, k):
        value = table[0]
        for i in range(1, BLOCKS):
            value = jnp.where(k == i, table[i], value)
        return value

    base_below = [keep[k] for k in range(BLOCKS)]
    base_above = [keep[k] + up[k - 1] for k in range(BLOCKS)]
    for j in range(CPR):
        home = homes[j]
        rank = jnp.int32(0)
        for i in range(j):
            rank = rank + jnp.where(homes[i] == home, 1, 0)
        kept = of(keep, home)
        after = rank - kept
        ups = of(up, home)
        stays = after < 0
        climbs = after < ups
        at = jnp.where(
            stays, KEPT + 1 + rank, jnp.where(climbs, UP + 1 + after, DOWN + 1 + after - ups)
        )
        out = jnp.where((block == home) & (lane == at), rows[j], out)
        above = lax.rem(home + 1, BLOCKS)
        below = lax.rem(home + BLOCKS - 1, BLOCKS)
        place[0, j] = jnp.where(stays, home, jnp.where(climbs, above, below))
        place[1, j] = jnp.where(
            stays,
            rank,
            jnp.where(climbs, of(base_below, above) + after, of(base_above, below) + after - ups),
        )
    plan[...] = out


def move_kernel(size, plan, keys, values, up_out, down_out, pool, up_stage, down_stage, sems):
    loads = [
        pltpu.make_async_copy(table, pool.at[i], sems.at[i])
        for i, table in enumerate((keys, values))
    ]
    for load in loads:
        load.start()
    for load in loads:
        load.wait()

    def fill(r, marks):
        ends = []
        for at, stage, mark in ((UP, up_stage, marks[0]), (DOWN, down_stage, marks[1])):
            for i in range(SLOTS):
                row = plan[r, at + 1 + i]
                stage[mark + i, 0] = pool[0, row]
                stage[mark + i, 1] = pool[1, row]
            ends.append(mark + plan[r, at])
        return tuple(ends)

    lax.fori_loop(0, plan.shape[0], fill, (jnp.int32(0), jnp.int32(0)))
    stores = [
        pltpu.make_async_copy(stage.at[pl.ds(0, size)], out, sems.at[i])
        for i, (stage, out) in enumerate(((up_stage, up_out), (down_stage, down_out)))
    ]
    for store in stores:
        store.start()
    for store in stores:
        store.wait()


def pick_kernel(shard_rows, size, plan, keys, values, below, above, send, pool, stage, sems, out_sem):
    loads = []
    for i, table in enumerate((keys, values)):
        loads.append(
            pltpu.make_async_copy(table, pool.at[i, pl.ds(0, shard_rows)], sems.at[i, 0])
        )
        for n, part in enumerate((below, above)):
            start = shard_rows + n * size
            loads.append(
                pltpu.make_async_copy(
                    part.at[:, i], pool.at[i, pl.ds(start, size)], sems.at[i, n + 1]
                )
            )
    for load in loads:
        load.start()
    for load in loads:
        load.wait()

    def fill(r, marks):
        kept = plan[r, KEPT]
        came = kept + plan[r, FROM_BELOW]
        for t in range(SLOTS):
            row = jnp.where(
                t < kept,
                plan[r, KEPT + 1 + t],
                jnp.where(t < came, marks[0] + t - kept, marks[1] + t - came),
            )
            stage[r, t, 0] = pool[0, row]
            stage[r, t, 1] = pool[1, row]
        pltpu.make_async_copy(stage.at[r], send.at[r], out_sem).start()
        return marks[0] + plan[r, FROM_BELOW], marks[1] + plan[r, FROM_ABOVE]

    first = (jnp.int32(shard_rows), jnp.int32(shard_rows + size))
    lax.fori_loop(0, send.shape[0], fill, first)
    pltpu.make_async_copy(stage, send, out_sem).wait()


def fresh_kernel(heads_kv, group, q, k, cosine, sine, q_out, k_out):
    cos = cosine[...]
    sin = sine[...]
    for h in range(heads_kv):
        cols = slice(h * HD, (h + 1) * HD)
        k_out[:, cols] = turn(k[:, cols].astype(jnp.float32), cos, sin).astype(jnp.bfloat16)
        for g in range(group):
            n = h * group + g
            turned = turn(q[:, n * HD : (n + 1) * HD].astype(jnp.float32), cos, sin)
            turned = turned.astype(jnp.bfloat16)
            for j in range(CPR):
                q_out[h * CPR + j, g * RPC : (g + 1) * RPC, :] = turned[j * RPC : (j + 1) * RPC]


def prepare_kernel(
    heads_kv,
    total_spans,
    place,
    span_lists,
    places_row,
    places_col,
    fresh_k,
    fresh_v,
    new_k,
    cos_span,
    sin_span,
    cos_token,
    sin_token,
    got,
    keys,
    vals,
    drift,
    kbuf,
    vbuf,
    key_stage,
    value_stage,
    sems,
    out_sem,
):
    copies = []
    for j in range(CPR):
        pair = [
            pltpu.make_async_copy(got.at[:, place[0, j], place[1, j], which], buf.at[j], sems.at[which, j])
            for which, buf in enumerate((kbuf, vbuf))
        ]
        for copy in pair:
            copy.start()
        copies.append(pair)
    width = fresh_k.shape[1]
    dest = lax.broadcasted_iota(jnp.int32, drift.shape, 0)
    lane = lax.broadcasted_iota(jnp.int32, drift.shape, 1)
    per_dest = total_spans // drift.shape[0]
    total = jnp.zeros(drift.shape, jnp.float32)
    token_row = lax.broadcasted_iota(jnp.int32, (CL, RPC), 0)
    token_lane = lax.broadcasted_iota(jnp.int32, (RPC, CL), 1)
    ones = jnp.ones((RPC, HD), jnp.bfloat16)
    stores = []
    for j in range(CPR):
        rows = slice(j * RPC, (j + 1) * RPC)
        span = slice(j * CL, (j + 1) * CL)
        take = (token_lane + j * CL == places_col[rows, :]).astype(jnp.float32)
        take = take.astype(jnp.bfloat16)
        put = (token_row + j * CL == places_row[j : j + 1, :]).astype(jnp.float32)
        put = put.astype(jnp.bfloat16)
        replaced = jnp.dot(put, ones, preferred_element_type=jnp.float32) > 0.5
        ca, sa = cos_span[j : j + 1, :], sin_span[j : j + 1, :]
        cb, sb = cos_token[...], sin_token[...]
        cos = ca * cb - sa * sb
        sin = sa * cb + ca * sb
        gap = jnp.zeros((RPC, width), jnp.float32)
        for copy, buf, fresh in zip(copies[j], (kbuf, vbuf), (fresh_k, fresh_v)):
            copy.wait()
            cached = jnp.dot(take, buf[j].reshape(CL, width), preferred_element_type=jnp.float32)
            delta = fresh[rows, :].astype(jnp.float32) - cached
            gap = gap + delta * delta
        share = jnp.sum(gap) * (1.0 / (2.0 * KVH * HD * RPC))
        chosen = span_lists[0, j]
        total = total + jnp.where(
            (dest == chosen // per_dest) & (lane == chosen % per_dest), share, 0.0
        )
        for h in range(heads_kv):
            cols = slice(h * HD, (h + 1) * HD)
            raw = kbuf[j, :, :, cols].reshape(CL, HD).astype(jnp.float32)
            new = jnp.dot(put, new_k[rows, cols], preferred_element_type=jnp.float32)
            ready = jnp.where(replaced, new, turn(raw, cos, sin))
            key_stage[j, h] = ready.astype(jnp.bfloat16)
            raw = vbuf[j, :, :, cols].reshape(CL, HD).astype(jnp.float32)
            new = jnp.dot(put, fresh_v[rows, cols], preferred_element_type=jnp.float32)
            value_stage[j, h] = jnp.where(replaced, new, raw).astype(jnp.bfloat16)
        for stage, whole in ((key_stage, keys), (value_stage, vals)):
            copy = pltpu.make_async_copy(stage.at[j], whole.at[:, span], out_sem)
            copy.start()
            stores.append(copy)
    drift[...] = total
    for copy in stores:
        copy.wait()


def attend_kernel(
    heads_kv, group, places_col, q, all_keys, all_vals, out, keys, vals, seen, scores, sems
):
    pairs = ((all_keys, keys), (all_vals, vals))
    for h in range(heads_kv):
        for which, (whole, buf) in enumerate(pairs):
            pltpu.make_async_copy(whole.at[h], buf.at[h], sems.at[which, h]).start()
    block = group * RPC
    token = lax.broadcasted_iota(jnp.int32, (RPC, CL), 1)
    for j in range(CPR):
        rows = slice(j * RPC, (j + 1) * RPC)
        seen[j] = jnp.where(token + j * CL <= places_col[rows, :], 0.0, -1e30)

    def head(h, carry):
        for which, (whole, buf) in enumerate(pairs):
            pltpu.make_async_copy(whole.at[h], buf.at[h], sems.at[which, h]).wait()
        for t in range(CPR):
            later = q[pl.ds(h * CPR + t, CPR - t)].reshape((CPR - t) * block, HD)
            scores[t * block :, t * CL : (t + 1) * CL] = lax.dot_general(
                later,
                keys[h, t * CL : (t + 1) * CL, :],
                (((1,), (1,)), ((), ())),
                preferred_element_type=jnp.float32,
            )
        for j in range(CPR):
            extent = (j + 1) * CL
            part = scores[j * block : (j + 1) * block, :extent]
            bias = jnp.concatenate([seen[j]] * group, axis=0)
            last = part[:, j * CL :] + bias
            part = last if j == 0 else jnp.concatenate([part[:, : j * CL], last], axis=1)
            row_max = jnp.max(part, axis=1, keepdims=True)
            weights = jnp.exp2((part - row_max) * SCALE_LOG2E)
            row_sum = jnp.sum(weights, axis=1, keepdims=True)
            mixed = jnp.dot(
                weights.astype(jnp.bfloat16),
                vals[h, :extent, :],
                preferred_element_type=jnp.float32,
            )
            mixed = (mixed / row_sum).astype(jnp.bfloat16)
            for g in range(group):
                start = pl.multiple_of((h * group + g) * HD, HD)
                out[j * RPC : (j + 1) * RPC, pl.ds(start, HD)] = mixed[g * RPC : (g + 1) * RPC]
        return carry

    lax.fori_loop(0, heads_kv, head, 0)


SMEM = pl.BlockSpec(memory_space=pltpu.SMEM)
VMEM = pl.BlockSpec(memory_space=pltpu.VMEM)
ANY = pl.BlockSpec(memory_space=pl.ANY)


def local(span_keys, span_values, span_row, span_lists, recompute_pos, fresh_q, fresh_k, fresh_v):
    n_store = lax.axis_size("store")
    n_req = lax.axis_size("req")
    n_tp = lax.axis_size("tp")
    n_all = n_store * n_req * n_tp
    peers = n_store * n_req
    shard_rows, tok_dev, width = span_keys.shape
    heads_kv = width // HD
    heads_q = fresh_q.shape[2] // HD
    group = heads_q // heads_kv
    bf16 = jnp.bfloat16

    def params(mebibytes):
        return pltpu.CompilerParams(vmem_limit_bytes=mebibytes << 20)


    assert n_req == BLOCKS and shard_rows * n_req == span_row.shape[0]
    plan, place = pl.pallas_call(
        functools.partial(ask_kernel, shard_rows),
        out_shape=(
            jax.ShapeDtypeStruct((peers, LANES), jnp.int32),
            jax.ShapeDtypeStruct((2, CPR), jnp.int32),
        ),
        in_specs=[SMEM, SMEM],
        out_specs=(VMEM, SMEM),
        name="ask",
    )(span_row, span_lists)
    plans = lax.all_to_all(plan, ("store", "req"), split_axis=0, concat_axis=0, tiled=True)
    piece = (2, tok_dev, width)
    climb = [(k, (k + 1) % n_req) for k in range(n_req)]
    sink = [(k, (k - 1) % n_req) for k in range(n_req)]

    def gather(size, plans, span_keys, span_values):
        moves = jax.ShapeDtypeStruct((size,) + piece, bf16)
        ups, downs = pl.pallas_call(
            functools.partial(move_kernel, size),
            out_shape=(moves, moves),
            in_specs=[SMEM, ANY, ANY],
            out_specs=(ANY, ANY),
            scratch_shapes=[
                pltpu.VMEM((2, shard_rows, tok_dev, width), bf16),
                pltpu.VMEM((size + SLOTS,) + piece, bf16),
                pltpu.VMEM((size + SLOTS,) + piece, bf16),
                pltpu.SemaphoreType.DMA((2,)),
            ],
            compiler_params=params(58),
            name="move",
        )(plans, span_keys, span_values)
        below = lax.ppermute(ups, "req", climb)
        above = lax.ppermute(downs, "req", sink)
        return pl.pallas_call(
            functools.partial(pick_kernel, shard_rows, size),
            out_shape=jax.ShapeDtypeStruct((peers, SLOTS) + piece, bf16),
            in_specs=[SMEM] + [ANY] * 4,
            out_specs=ANY,
            scratch_shapes=[
                pltpu.VMEM((2, shard_rows + 2 * size, tok_dev, width), bf16),
                pltpu.VMEM((peers, SLOTS) + piece, bf16),
                pltpu.SemaphoreType.DMA((2, 3)),
                pltpu.SemaphoreType.DMA,
            ],
            compiler_params=params(58),
            name="pick",
        )(plans, span_keys, span_values, below, above)

    load = jnp.max(jnp.sum(plans[:, LOADS : LOADS + 2 * BLOCKS], axis=0))
    level = sum((load > size).astype(jnp.int32) for size in SIZES)
    most = SLOTS * peers
    send = lax.switch(
        level,
        [functools.partial(gather, size) for size in SIZES + (most,)],
        plans,
        span_keys,
        span_values,
    )
    got = lax.all_to_all(send, ("store", "req"), split_axis=0, concat_axis=0, tiled=True)
    got = got.reshape((n_store, n_req, SLOTS) + piece)

    places, raw_q, raw_k, _ = lax.optimization_barrier((recompute_pos, fresh_q, fresh_k, send))
    places = places[0]
    raw_k = raw_k[0]
    new_v = fresh_v[0]
    angles = places.astype(jnp.float32)[:, None] * jnp.asarray(FREQ)[None, :]
    cosine = jnp.cos(angles)
    sine = jnp.sin(angles)
    queries, new_k = pl.pallas_call(
        functools.partial(fresh_kernel, heads_kv, group),
        out_shape=(
            jax.ShapeDtypeStruct((heads_kv * CPR, group * RPC, HD), bf16),
            jax.ShapeDtypeStruct((RC, width), bf16),
        ),
        in_specs=[VMEM] * 4,
        out_specs=(VMEM, VMEM),
        compiler_params=params(16),
        name="fresh",
    )(
        raw_q[0],
        raw_k,
        jnp.concatenate([cosine, cosine], axis=1),
        jnp.concatenate([-sine, sine], axis=1),
    )
    places_col = places[:, None]
    places_row = places.reshape(CPR, RPC)

    keys, vals, part = pl.pallas_call(
        functools.partial(prepare_kernel, heads_kv, span_row.shape[0]),
        out_shape=(
            jax.ShapeDtypeStruct((heads_kv, CTX, HD), bf16),
            jax.ShapeDtypeStruct((heads_kv, CTX, HD), bf16),
            jax.ShapeDtypeStruct((n_all, LANES), jnp.float32),
        ),
        in_specs=[SMEM, SMEM] + [VMEM] * 9 + [ANY],
        out_specs=(ANY, ANY, VMEM),
        scratch_shapes=[
            pltpu.VMEM((CPR, n_store, tok_dev, width), bf16),
            pltpu.VMEM((CPR, n_store, tok_dev, width), bf16),
            pltpu.VMEM((CPR, heads_kv, CL, HD), bf16),
            pltpu.VMEM((CPR, heads_kv, CL, HD), bf16),
            pltpu.SemaphoreType.DMA((2, CPR)),
            pltpu.SemaphoreType.DMA,
        ],
        compiler_params=params(52),
        cost_estimate=pl.CostEstimate(
            flops=8 * RC * CTX * width // CPR, bytes_accessed=8 * CTX * width, transcendentals=0
        ),
        name="prepare",
    )(
        place,
        span_lists,
        places_row,
        places_col,
        raw_k,
        new_v,
        new_k,
        jnp.asarray(COS_SPAN),
        jnp.asarray(SIN_SPAN),
        jnp.asarray(COS_TOKEN),
        jnp.asarray(SIN_TOKEN),
        got,
    )
    parts = lax.all_to_all(part, ("store", "req", "tp"), split_axis=0, concat_axis=0, tiled=True)

    attended = pl.pallas_call(
        functools.partial(attend_kernel, heads_kv, group),
        out_shape=jax.ShapeDtypeStruct((RC, heads_q * HD), bf16),
        in_specs=[VMEM, VMEM, ANY, ANY],
        out_specs=VMEM,
        scratch_shapes=[
            pltpu.VMEM((heads_kv, CTX, HD), bf16),
            pltpu.VMEM((heads_kv, CTX, HD), bf16),
            pltpu.VMEM((CPR, RPC, CL), jnp.float32),
            pltpu.VMEM((CPR * group * RPC, CTX), jnp.float32),
            pltpu.SemaphoreType.DMA((2, heads_kv)),
        ],
        compiler_params=params(59),
        cost_estimate=pl.CostEstimate(
            flops=2 * heads_q * RC * CTX * HD * 2,
            bytes_accessed=4 * CTX * width + 4 * RC * heads_q * HD,
            transcendentals=heads_q * RC * CTX // 2,
        ),
        name="attend",
    )(places_col, queries, keys, vals)
    per_dest = span_row.shape[0] // n_all
    drift_part = jnp.sum(parts, axis=0)[:per_dest]
    return (attended[None], drift_part)


def solution(mesh):
    in_specs = (
        P("req", "store", "tp"),
        P("req", "store", "tp"),
        P(),
        P(("store", "req"), None),
        P(("store", "req"), None),
        P(("store", "req"), None, "tp"),
        P(("store", "req"), None, "tp"),
        P(("store", "req"), None, "tp"),
    )
    out_specs = (P(("store", "req"), None, "tp"), P(("store", "req", "tp")))
    return jax.shard_map(local, mesh=mesh, in_specs=in_specs, out_specs=out_specs, check_vma=False)
```

```python
import functools

import jax
import jax.numpy as jnp
import numpy as np
from jax import lax
from jax.experimental import pallas as pl
from jax.experimental.pallas import tpu as pltpu
from jax.sharding import PartitionSpec as P

HD = 128
HALF = HD // 2
CPR = 8
RPC = 16
CL = 256
CTX = CPR * CL
RC = CPR * RPC
KVH = 8
BLOCKS = 4
SLOTS = CPR // BLOCKS
SIZES = (25, 29, 36)
KEPT, UP, DOWN, FROM_BELOW, FROM_ABOVE, LOADS = 0, 4, 8, 12, 13, 16
LANES = 128
SCALE_LOG2E = float(HD ** -0.5 * np.log2(np.e))

FREQ = np.exp(-np.log(500000.0) * np.arange(HALF) / HALF).astype(np.float32)


def angle_tables(positions):
    angles = positions[:, None].astype(np.float64) * FREQ[None, :].astype(np.float64)
    cosine = np.cos(angles).astype(np.float32)
    sine = np.sin(angles).astype(np.float32)
    return (
        np.concatenate([cosine, cosine], axis=1),
        np.concatenate([-sine, sine], axis=1),
    )


COS_SPAN, SIN_SPAN = angle_tables(CL * np.arange(CPR))
COS_TOKEN, SIN_TOKEN = angle_tables(np.arange(CL))


def turn(x, cosine, sine):
    return x * cosine + pltpu.roll(x, HALF, 1) * sine


def ask_kernel(shard_rows, span_row, span_lists, plan, place):
    spans = [span_row[span_lists[0, j]] for j in range(CPR)]
    homes = [row // shard_rows for row in spans]
    rows = [row % shard_rows for row in spans]
    one = [[jnp.where(home == k, 1, 0) for home in homes] for k in range(BLOCKS)]
    counts = [sum(one[k]) for k in range(BLOCKS)]
    sums = []
    total = jnp.int32(0)
    for k in range(BLOCKS):
        total = total + counts[k] - SLOTS
        sums.append(total)
    low, high = jnp.minimum(sums[0], sums[1]), jnp.maximum(sums[0], sums[1])
    low2, high2 = jnp.minimum(sums[2], sums[3]), jnp.maximum(sums[2], sums[3])
    middle, middle2 = jnp.maximum(low, low2), jnp.minimum(high, high2)
    first, second = jnp.minimum(middle, middle2), jnp.maximum(middle, middle2)
    whole = sums[0] + sums[1] + sums[2] + sums[3]
    mixed = lax.rem(sum(span_lists[0, j] for j in range(CPR)), 4) == 0
    level = jnp.abs(whole - BLOCKS * first) <= jnp.abs(whole - BLOCKS * second)
    shift = jnp.where(level != mixed, first, second)
    flow = [x - shift for x in sums]
    up = [jnp.maximum(x, 0) for x in flow]
    down = [jnp.maximum(-flow[k - 1], 0) for k in range(BLOCKS)]
    keep = [counts[k] - up[k] - down[k] for k in range(BLOCKS)]

    block = lax.broadcasted_iota(jnp.int32, plan.shape, 0) % BLOCKS
    lane = lax.broadcasted_iota(jnp.int32, plan.shape, 1)
    out = jnp.zeros(plan.shape, jnp.int32)
    for k in range(BLOCKS):
        own = block == k
        heads = (
            (KEPT, keep[k]),
            (UP, up[k]),
            (DOWN, down[k]),
            (FROM_BELOW, up[k - 1]),
            (FROM_ABOVE, down[(k + 1) % BLOCKS]),
        )
        for at, value in heads:
            out = jnp.where(own & (lane == at), value, out)
        out = jnp.where(lane == LOADS + k, up[k], out)
        out = jnp.where(lane == LOADS + BLOCKS + k, down[k], out)

    def of(table, k):
        value = table[0]
        for i in range(1, BLOCKS):
            value = jnp.where(k == i, table[i], value)
        return value

    base_below = [keep[k] for k in range(BLOCKS)]
    base_above = [keep[k] + up[k - 1] for k in range(BLOCKS)]
    for j in range(CPR):
        home = homes[j]
        rank = jnp.int32(0)
        for i in range(j):
            rank = rank + jnp.where(homes[i] == home, 1, 0)
        kept = of(keep, home)
        after = rank - kept
        ups = of(up, home)
        stays = after < 0
        climbs = after < ups
        at = jnp.where(
            stays, KEPT + 1 + rank, jnp.where(climbs, UP + 1 + after, DOWN + 1 + after - ups)
        )
        out = jnp.where((block == home) & (lane == at), rows[j], out)
        above = lax.rem(home + 1, BLOCKS)
        below = lax.rem(home + BLOCKS - 1, BLOCKS)
        place[0, j] = jnp.where(stays, home, jnp.where(climbs, above, below))
        place[1, j] = jnp.where(
            stays,
            rank,
            jnp.where(climbs, of(base_below, above) + after, of(base_above, below) + after - ups),
        )
    plan[...] = out


def move_kernel(size, plan, table, up_out, down_out, rows, up_stage, down_stage, sems):
    load = pltpu.make_async_copy(table, rows, sems.at[0])
    load.start()
    load.wait()

    def fill(r, marks):
        ends = []
        for at, stage, mark in ((UP, up_stage, marks[0]), (DOWN, down_stage, marks[1])):
            for i in range(SLOTS):
                stage[mark + i] = rows[plan[r, at + 1 + i]]
            ends.append(mark + plan[r, at])
        return tuple(ends)

    lax.fori_loop(0, plan.shape[0], fill, (jnp.int32(0), jnp.int32(0)), unroll=4)
    stores = [
        pltpu.make_async_copy(stage.at[pl.ds(0, size)], out, sems.at[i])
        for i, (stage, out) in enumerate(((up_stage, up_out), (down_stage, down_out)))
    ]
    for store in stores:
        store.start()
    for store in stores:
        store.wait()


def own_kernel(plan, keys, values, send, pool, stage, sems, out_sem):
    loads = [
        pltpu.make_async_copy(table, pool.at[i], sems.at[i])
        for i, table in enumerate((keys, values))
    ]
    for load in loads:
        load.start()
    for load in loads:
        load.wait()

    def fill(r, carry):
        for t in range(SLOTS):
            row = plan[r, KEPT + 1 + t]
            stage[r, t, 0] = pool[0, row]
            stage[r, t, 1] = pool[1, row]
        pltpu.make_async_copy(stage.at[r], send.at[r], out_sem).start()
        return carry

    lax.fori_loop(0, send.shape[0], fill, 0, unroll=4)
    pltpu.make_async_copy(stage, send, out_sem).wait()


def patch_kernel(plan, below_k, above_k, below_v, above_v, own, send, sem):
    def fill(r, marks):
        kept = plan[r, KEPT]
        second = kept + plan[r, FROM_BELOW]
        for t in range(SLOTS):

            @pl.when((t >= kept) & (t < second))
            def _():
                row = marks[0] + t - kept
                pltpu.make_async_copy(below_k.at[row], send.at[r, t, 0], sem).start()
                pltpu.make_async_copy(below_v.at[row], send.at[r, t, 1], sem).start()

            @pl.when(t >= second)
            def _():
                row = marks[1] + t - second
                pltpu.make_async_copy(above_k.at[row], send.at[r, t, 0], sem).start()
                pltpu.make_async_copy(above_v.at[row], send.at[r, t, 1], sem).start()

        return marks[0] + plan[r, FROM_BELOW], marks[1] + plan[r, FROM_ABOVE]

    ends = lax.fori_loop(0, send.shape[0], fill, (jnp.int32(0), jnp.int32(0)), unroll=4)

    def drain(i, carry):
        pltpu.make_async_copy(send.at[0, 0], send.at[0, 0], sem).wait()
        return carry

    lax.fori_loop(0, ends[0] + ends[1], drain, 0)


def fresh_kernel(heads_kv, group, q, k, cosine, sine, q_out, k_out):
    cos = cosine[...]
    sin = sine[...]
    for h in range(heads_kv):
        cols = slice(h * HD, (h + 1) * HD)
        k_out[:, cols] = turn(k[:, cols].astype(jnp.float32), cos, sin).astype(jnp.bfloat16)
        for g in range(group):
            n = h * group + g
            turned = turn(q[:, n * HD : (n + 1) * HD].astype(jnp.float32), cos, sin)
            turned = turned.astype(jnp.bfloat16)
            for j in range(CPR):
                q_out[h * CPR + j, g * RPC : (g + 1) * RPC, :] = turned[j * RPC : (j + 1) * RPC]


def drift_kernel(
    total_spans, place, span_lists, places_col, fresh_k, fresh_v, got, drift, kbuf, vbuf, sems
):
    copies = []
    for j in range(CPR):
        for which, buf in enumerate((kbuf, vbuf)):
            copy = pltpu.make_async_copy(
                got.at[:, place[0, j], place[1, j], which], buf.at[j], sems.at[which, j]
            )
            copy.start()
            copies.append(copy)
    width = fresh_k.shape[1]
    dest = lax.broadcasted_iota(jnp.int32, drift.shape, 0)
    lane = lax.broadcasted_iota(jnp.int32, drift.shape, 1)
    per_dest = total_spans // drift.shape[0]
    token = lax.broadcasted_iota(jnp.int32, (RPC, CL), 1)
    total = jnp.zeros(drift.shape, jnp.float32)
    for j in range(CPR):
        rows = slice(j * RPC, (j + 1) * RPC)
        take = (token + j * CL == places_col[rows, :]).astype(jnp.float32)
        take = take.astype(jnp.bfloat16)
        gap = jnp.zeros((RPC, width), jnp.float32)
        copies[2 * j].wait()
        copies[2 * j + 1].wait()
        for buf, fresh in ((kbuf, fresh_k), (vbuf, fresh_v)):
            cached = jnp.dot(take, buf[j].reshape(CL, width), preferred_element_type=jnp.float32)
            delta = fresh[rows, :].astype(jnp.float32) - cached
            gap = gap + delta * delta
        share = jnp.sum(gap) * (1.0 / (2.0 * KVH * HD * RPC))
        chosen = span_lists[0, j]
        total = total + jnp.where(
            (dest == chosen // per_dest) & (lane == chosen % per_dest), share, 0.0
        )
    drift[...] = total


def attend_kernel(
    heads_kv,
    group,
    place,
    places_row,
    places_col,
    q,
    new_k,
    new_v,
    cos_span,
    sin_span,
    cos_token,
    sin_token,
    got,
    out,
    raw,
    keys,
    vals,
    seen,
    put,
    stay,
    cosine,
    sine,
    scores,
    sems,
):
    def loads(h, slot):
        cols = pl.ds(pl.multiple_of(h * HD, HD), HD)
        return [
            pltpu.make_async_copy(
                got.at[:, place[0, j], place[1, j], which, :, cols],
                raw.at[slot, which, j],
                sems.at[slot],
            )
            for which in range(2)
            for j in range(CPR)
        ]

    for load in loads(0, 0):
        load.start()
    block = group * RPC
    token_lane = lax.broadcasted_iota(jnp.int32, (RPC, CL), 1)
    token_row = lax.broadcasted_iota(jnp.int32, (CL, RPC), 0)
    ones = jnp.ones((RPC, HD), jnp.bfloat16)
    for j in range(CPR):
        rows = slice(j * RPC, (j + 1) * RPC)
        span = slice(j * CL, (j + 1) * CL)
        seen[j] = jnp.where(token_lane + j * CL <= places_col[rows, :], 0.0, -1e30)
        hits = (token_row + j * CL == places_row[j : j + 1, :]).astype(jnp.float32)
        hits = hits.astype(jnp.bfloat16)
        put[j] = hits
        stay[span, :] = 1.0 - jnp.dot(hits, ones, preferred_element_type=jnp.float32)
        ca, sa = cos_span[j : j + 1, :], sin_span[j : j + 1, :]
        cb, sb = cos_token[...], sin_token[...]
        cosine[span, :] = ca * cb - sa * sb
        sine[span, :] = sa * cb + ca * sb

    def head(h, carry):
        slot = lax.rem(h, 2)
        cols = pl.ds(pl.multiple_of(h * HD, HD), HD)
        pltpu.make_async_copy(raw.at[slot], raw.at[slot], sems.at[slot]).wait()

        @pl.when(h + 1 < heads_kv)
        def _():
            for load in loads(h + 1, 1 - slot):
                load.start()

        for j in range(CPR):
            rows = slice(j * RPC, (j + 1) * RPC)
            span = slice(j * CL, (j + 1) * CL)
            old = raw[slot, 0, j].reshape(CL, HD).astype(jnp.float32)
            new = jnp.dot(put[j], new_k[rows, cols], preferred_element_type=jnp.float32)
            old = turn(old, cosine[span, :], sine[span, :])
            keys[span, :] = (old * stay[span, :] + new).astype(jnp.bfloat16)
            old = raw[slot, 1, j].reshape(CL, HD).astype(jnp.float32)
            new = jnp.dot(put[j], new_v[rows, cols], preferred_element_type=jnp.float32)
            vals[span, :] = (old * stay[span, :] + new).astype(jnp.bfloat16)
        for t in range(CPR):
            later = q[pl.ds(h * CPR + t, CPR - t)].reshape((CPR - t) * block, HD)
            scores[t * block :, t * CL : (t + 1) * CL] = lax.dot_general(
                later,
                keys[t * CL : (t + 1) * CL, :],
                (((1,), (1,)), ((), ())),
                preferred_element_type=jnp.float32,
            )
        for j in range(CPR):
            extent = (j + 1) * CL
            part = scores[j * block : (j + 1) * block, :extent]
            bias = jnp.concatenate([seen[j]] * group, axis=0)
            last = part[:, j * CL :] + bias
            part = last if j == 0 else jnp.concatenate([part[:, : j * CL], last], axis=1)
            row_max = jnp.max(part, axis=1, keepdims=True)
            weights = jnp.exp2((part - row_max) * SCALE_LOG2E)
            row_sum = jnp.sum(weights, axis=1, keepdims=True)
            mixed = jnp.dot(
                weights.astype(jnp.bfloat16),
                vals[:extent, :],
                preferred_element_type=jnp.float32,
            )
            mixed = (mixed / row_sum).astype(jnp.bfloat16)
            for g in range(group):
                start = pl.multiple_of((h * group + g) * HD, HD)
                out[j * RPC : (j + 1) * RPC, pl.ds(start, HD)] = mixed[g * RPC : (g + 1) * RPC]
        return carry

    lax.fori_loop(0, heads_kv, head, 0)


SMEM = pl.BlockSpec(memory_space=pltpu.SMEM)
VMEM = pl.BlockSpec(memory_space=pltpu.VMEM)
ANY = pl.BlockSpec(memory_space=pl.ANY)


def local(span_keys, span_values, span_row, span_lists, recompute_pos, fresh_q, fresh_k, fresh_v):
    n_store = lax.axis_size("store")
    n_req = lax.axis_size("req")
    n_tp = lax.axis_size("tp")
    n_all = n_store * n_req * n_tp
    peers = n_store * n_req
    shard_rows, tok_dev, width = span_keys.shape
    heads_kv = width // HD
    heads_q = fresh_q.shape[2] // HD
    group = heads_q // heads_kv
    bf16 = jnp.bfloat16

    def params(mebibytes):
        return pltpu.CompilerParams(vmem_limit_bytes=mebibytes << 20)


    assert n_req == BLOCKS and shard_rows * n_req == span_row.shape[0]
    plan, place = pl.pallas_call(
        functools.partial(ask_kernel, shard_rows),
        out_shape=(
            jax.ShapeDtypeStruct((peers, LANES), jnp.int32),
            jax.ShapeDtypeStruct((2, CPR), jnp.int32),
        ),
        in_specs=[SMEM, SMEM],
        out_specs=(VMEM, SMEM),
        name="ask",
    )(span_row, span_lists)
    plans = lax.all_to_all(plan, ("store", "req"), split_axis=0, concat_axis=0, tiled=True)
    piece = (2, tok_dev, width)
    climb = [(k, (k + 1) % n_req) for k in range(n_req)]
    sink = [(k, (k - 1) % n_req) for k in range(n_req)]

    def gather(size, plans, span_keys, span_values):
        moves = jax.ShapeDtypeStruct((size, tok_dev, width), bf16)
        move = pl.pallas_call(
            functools.partial(move_kernel, size),
            out_shape=(moves, moves),
            in_specs=[SMEM, ANY],
            out_specs=(ANY, ANY),
            scratch_shapes=[
                pltpu.VMEM((shard_rows, tok_dev, width), bf16),
                pltpu.VMEM((size + SLOTS, tok_dev, width), bf16),
                pltpu.VMEM((size + SLOTS, tok_dev, width), bf16),
                pltpu.SemaphoreType.DMA((2,)),
            ],
            compiler_params=params(60),
            name="move",
        )
        came = []
        for table in (span_keys, span_values):
            ups, downs = move(plans, table)
            came.append(lax.ppermute(ups, "req", climb))
            came.append(lax.ppermute(downs, "req", sink))
            plans, span_keys, span_values, _ = lax.optimization_barrier(
                (plans, span_keys, span_values, ups)
            )
        own = pl.pallas_call(
            own_kernel,
            out_shape=jax.ShapeDtypeStruct((peers, SLOTS) + piece, bf16),
            in_specs=[SMEM, ANY, ANY],
            out_specs=ANY,
            scratch_shapes=[
                pltpu.VMEM((2, shard_rows, tok_dev, width), bf16),
                pltpu.VMEM((peers, SLOTS) + piece, bf16),
                pltpu.SemaphoreType.DMA((2,)),
                pltpu.SemaphoreType.DMA,
            ],
            compiler_params=params(58),
            name="own",
        )(plans, span_keys, span_values)
        return pl.pallas_call(
            patch_kernel,
            out_shape=jax.ShapeDtypeStruct((peers, SLOTS) + piece, bf16),
            in_specs=[SMEM] + [VMEM] * 4 + [ANY],
            out_specs=ANY,
            scratch_shapes=[pltpu.SemaphoreType.DMA],
            input_output_aliases={5: 0},
            compiler_params=params(40),
            name="patch",
        )(plans, *came, own)

    load = jnp.max(jnp.sum(plans[:, LOADS : LOADS + 2 * BLOCKS], axis=0))
    level = sum((load > size).astype(jnp.int32) for size in SIZES)
    most = SLOTS * peers
    send = lax.switch(
        level,
        [functools.partial(gather, size) for size in SIZES + (most,)],
        plans,
        span_keys,
        span_values,
    )
    got = lax.all_to_all(send, ("store", "req"), split_axis=0, concat_axis=0, tiled=True)
    got = got.reshape((n_store, n_req, SLOTS) + piece)

    places, raw_q, raw_k, _ = lax.optimization_barrier((recompute_pos, fresh_q, fresh_k, send))
    places = places[0]
    raw_k = raw_k[0]
    new_v = fresh_v[0]
    angles = places.astype(jnp.float32)[:, None] * jnp.asarray(FREQ)[None, :]
    cosine = jnp.cos(angles)
    sine = jnp.sin(angles)
    queries, new_k = pl.pallas_call(
        functools.partial(fresh_kernel, heads_kv, group),
        out_shape=(
            jax.ShapeDtypeStruct((heads_kv * CPR, group * RPC, HD), bf16),
            jax.ShapeDtypeStruct((RC, width), bf16),
        ),
        in_specs=[VMEM] * 4,
        out_specs=(VMEM, VMEM),
        compiler_params=params(16),
        name="fresh",
    )(
        raw_q[0],
        raw_k,
        jnp.concatenate([cosine, cosine], axis=1),
        jnp.concatenate([-sine, sine], axis=1),
    )
    places_col = places[:, None]
    places_row = places.reshape(CPR, RPC)

    part = pl.pallas_call(
        functools.partial(drift_kernel, span_row.shape[0]),
        out_shape=jax.ShapeDtypeStruct((n_all, LANES), jnp.float32),
        in_specs=[SMEM, SMEM, VMEM, VMEM, VMEM, ANY],
        out_specs=VMEM,
        scratch_shapes=[
            pltpu.VMEM((CPR, n_store, tok_dev, width), bf16),
            pltpu.VMEM((CPR, n_store, tok_dev, width), bf16),
            pltpu.SemaphoreType.DMA((2, CPR)),
        ],
        compiler_params=params(58),
        cost_estimate=pl.CostEstimate(
            flops=4 * RC * CL * width, bytes_accessed=4 * CTX * width, transcendentals=0
        ),
        name="drift",
    )(place, span_lists, places_col, raw_k, new_v, got)
    parts = lax.all_to_all(part, ("store", "req", "tp"), split_axis=0, concat_axis=0, tiled=True)

    attended = pl.pallas_call(
        functools.partial(attend_kernel, heads_kv, group),
        out_shape=jax.ShapeDtypeStruct((RC, heads_q * HD), bf16),
        in_specs=[SMEM] + [VMEM] * 9 + [ANY],
        out_specs=VMEM,
        scratch_shapes=[
            pltpu.VMEM((2, 2, CPR, n_store, tok_dev, HD), bf16),
            pltpu.VMEM((CTX, HD), bf16),
            pltpu.VMEM((CTX, HD), bf16),
            pltpu.VMEM((CPR, RPC, CL), jnp.float32),
            pltpu.VMEM((CPR, CL, RPC), bf16),
            pltpu.VMEM((CTX, HD), jnp.float32),
            pltpu.VMEM((CTX, HD), jnp.float32),
            pltpu.VMEM((CTX, HD), jnp.float32),
            pltpu.VMEM((CPR * group * RPC, CTX), jnp.float32),
            pltpu.SemaphoreType.DMA((2,)),
        ],
        compiler_params=params(58),
        cost_estimate=pl.CostEstimate(
            flops=2 * heads_q * RC * CTX * HD * 2,
            bytes_accessed=4 * CTX * width + 4 * RC * heads_q * HD,
            transcendentals=heads_q * RC * CTX // 2,
        ),
        name="attend",
    )(
        place,
        places_row,
        places_col,
        queries,
        new_k,
        new_v,
        jnp.asarray(COS_SPAN),
        jnp.asarray(SIN_SPAN),
        jnp.asarray(COS_TOKEN),
        jnp.asarray(SIN_TOKEN),
        got,
    )
    per_dest = span_row.shape[0] // n_all
    drift_part = jnp.sum(parts, axis=0)[:per_dest]
    return (attended[None], drift_part)


def solution(mesh):
    in_specs = (
        P("req", "store", "tp"),
        P("req", "store", "tp"),
        P(),
        P(("store", "req"), None),
        P(("store", "req"), None),
        P(("store", "req"), None, "tp"),
        P(("store", "req"), None, "tp"),
        P(("store", "req"), None, "tp"),
    )
    out_specs = (P(("store", "req"), None, "tp"), P(("store", "req", "tp")))
    return jax.shard_map(local, mesh=mesh, in_specs=in_specs, out_specs=out_specs, check_vma=False)
```

```python
import functools

import jax
import jax.numpy as jnp
import numpy as np
from jax import lax
from jax.experimental import pallas as pl
from jax.experimental.pallas import tpu as pltpu
from jax.sharding import PartitionSpec as P

HD = 128
HALF = HD // 2
CPR = 8
RPC = 16
CL = 256
CTX = CPR * CL
RC = CPR * RPC
KVH = 8
BLOCKS = 4
SLOTS = CPR // BLOCKS
SIZES = (25, 29, 36)
KEPT, UP, DOWN, FROM_BELOW, FROM_ABOVE, LOADS = 0, 4, 8, 12, 13, 16
LANES = 128
SCALE_LOG2E = float(HD ** -0.5 * np.log2(np.e))

FREQ = np.exp(-np.log(500000.0) * np.arange(HALF) / HALF).astype(np.float32)


def angle_tables(positions):
    angles = positions[:, None].astype(np.float64) * FREQ[None, :].astype(np.float64)
    cosine = np.cos(angles).astype(np.float32)
    sine = np.sin(angles).astype(np.float32)
    return (
        np.concatenate([cosine, cosine], axis=1),
        np.concatenate([-sine, sine], axis=1),
    )


COS_SPAN, SIN_SPAN = angle_tables(CL * np.arange(CPR))
COS_TOKEN, SIN_TOKEN = angle_tables(np.arange(CL))


def turn(x, cosine, sine):
    return x * cosine + pltpu.roll(x, HALF, 1) * sine


def ask_kernel(shard_rows, span_row, span_lists, plan, place):
    spans = [span_row[span_lists[0, j]] for j in range(CPR)]
    homes = [row // shard_rows for row in spans]
    rows = [row % shard_rows for row in spans]
    one = [[jnp.where(home == k, 1, 0) for home in homes] for k in range(BLOCKS)]
    counts = [sum(one[k]) for k in range(BLOCKS)]
    sums = []
    total = jnp.int32(0)
    for k in range(BLOCKS):
        total = total + counts[k] - SLOTS
        sums.append(total)
    low, high = jnp.minimum(sums[0], sums[1]), jnp.maximum(sums[0], sums[1])
    low2, high2 = jnp.minimum(sums[2], sums[3]), jnp.maximum(sums[2], sums[3])
    middle, middle2 = jnp.maximum(low, low2), jnp.minimum(high, high2)
    first, second = jnp.minimum(middle, middle2), jnp.maximum(middle, middle2)
    whole = sums[0] + sums[1] + sums[2] + sums[3]
    mixed = lax.rem(sum(span_lists[0, j] for j in range(CPR)), 4) == 0
    level = jnp.abs(whole - BLOCKS * first) <= jnp.abs(whole - BLOCKS * second)
    shift = jnp.where(level != mixed, first, second)
    flow = [x - shift for x in sums]
    up = [jnp.maximum(x, 0) for x in flow]
    down = [jnp.maximum(-flow[k - 1], 0) for k in range(BLOCKS)]
    keep = [counts[k] - up[k] - down[k] for k in range(BLOCKS)]

    block = lax.broadcasted_iota(jnp.int32, plan.shape, 0) % BLOCKS
    lane = lax.broadcasted_iota(jnp.int32, plan.shape, 1)
    out = jnp.zeros(plan.shape, jnp.int32)
    for k in range(BLOCKS):
        own = block == k
        heads = (
            (KEPT, keep[k]),
            (UP, up[k]),
            (DOWN, down[k]),
            (FROM_BELOW, up[k - 1]),
            (FROM_ABOVE, down[(k + 1) % BLOCKS]),
        )
        for at, value in heads:
            out = jnp.where(own & (lane == at), value, out)
        out = jnp.where(lane == LOADS + k, up[k], out)
        out = jnp.where(lane == LOADS + BLOCKS + k, down[k], out)

    def of(table, k):
        value = table[0]
        for i in range(1, BLOCKS):
            value = jnp.where(k == i, table[i], value)
        return value

    base_below = [keep[k] for k in range(BLOCKS)]
    base_above = [keep[k] + up[k - 1] for k in range(BLOCKS)]
    for j in range(CPR):
        home = homes[j]
        rank = jnp.int32(0)
        for i in range(j):
            rank = rank + jnp.where(homes[i] == home, 1, 0)
        kept = of(keep, home)
        after = rank - kept
        ups = of(up, home)
        stays = after < 0
        climbs = after < ups
        at = jnp.where(
            stays, KEPT + 1 + rank, jnp.where(climbs, UP + 1 + after, DOWN + 1 + after - ups)
        )
        out = jnp.where((block == home) & (lane == at), rows[j], out)
        above = lax.rem(home + 1, BLOCKS)
        below = lax.rem(home + BLOCKS - 1, BLOCKS)
        place[0, j] = jnp.where(stays, home, jnp.where(climbs, above, below))
        place[1, j] = jnp.where(
            stays,
            rank,
            jnp.where(climbs, of(base_below, above) + after, of(base_above, below) + after - ups),
        )
    plan[...] = out


def move_kernel(size, plan, table, up_out, down_out, rows, up_stage, down_stage, sems):
    load = pltpu.make_async_copy(table, rows, sems.at[0])
    load.start()
    load.wait()

    def fill(r, marks):
        ends = []
        for at, stage, mark in ((UP, up_stage, marks[0]), (DOWN, down_stage, marks[1])):
            for i in range(SLOTS):
                stage[mark + i] = rows[plan[r, at + 1 + i]]
            ends.append(mark + plan[r, at])
        return tuple(ends)

    lax.fori_loop(0, plan.shape[0], fill, (jnp.int32(0), jnp.int32(0)), unroll=4)
    stores = [
        pltpu.make_async_copy(stage.at[pl.ds(0, size)], out, sems.at[i])
        for i, (stage, out) in enumerate(((up_stage, up_out), (down_stage, down_out)))
    ]
    for store in stores:
        store.start()
    for store in stores:
        store.wait()


def own_kernel(plan, keys, values, send, pool, stage, sems, out_sem):
    loads = [
        pltpu.make_async_copy(table, pool.at[i], sems.at[i])
        for i, table in enumerate((keys, values))
    ]
    for load in loads:
        load.start()
    for load in loads:
        load.wait()

    def fill(r, carry):
        for t in range(SLOTS):
            row = plan[r, KEPT + 1 + t]
            stage[r, t, 0] = pool[0, row]
            stage[r, t, 1] = pool[1, row]
        pltpu.make_async_copy(stage.at[r], send.at[r], out_sem).start()
        return carry

    lax.fori_loop(0, send.shape[0], fill, 0, unroll=4)
    pltpu.make_async_copy(stage, send, out_sem).wait()


def patch_kernel(plan, below_k, above_k, below_v, above_v, own, send, sem):
    def fill(r, marks):
        kept = plan[r, KEPT]
        second = kept + plan[r, FROM_BELOW]
        for t in range(SLOTS):

            @pl.when((t >= kept) & (t < second))
            def _():
                row = marks[0] + t - kept
                pltpu.make_async_copy(below_k.at[row], send.at[r, t, 0], sem).start()
                pltpu.make_async_copy(below_v.at[row], send.at[r, t, 1], sem).start()

            @pl.when(t >= second)
            def _():
                row = marks[1] + t - second
                pltpu.make_async_copy(above_k.at[row], send.at[r, t, 0], sem).start()
                pltpu.make_async_copy(above_v.at[row], send.at[r, t, 1], sem).start()

        return marks[0] + plan[r, FROM_BELOW], marks[1] + plan[r, FROM_ABOVE]

    ends = lax.fori_loop(0, send.shape[0], fill, (jnp.int32(0), jnp.int32(0)), unroll=4)

    def drain(i, carry):
        pltpu.make_async_copy(send.at[0, 0], send.at[0, 0], sem).wait()
        return carry

    lax.fori_loop(0, ends[0] + ends[1], drain, 0)


def fresh_kernel(heads_kv, group, q, k, v, cosine, sine, q_out, pair_out):
    cos = cosine[...]
    sin = sine[...]
    for h in range(heads_kv):
        cols = slice(h * HD, (h + 1) * HD)
        turned = turn(k[:, cols].astype(jnp.float32), cos, sin)
        pair_out[h, :, :HD] = turned.astype(jnp.bfloat16)
        pair_out[h, :, HD:] = v[:, cols]
        for g in range(group):
            n = h * group + g
            turned = turn(q[:, n * HD : (n + 1) * HD].astype(jnp.float32), cos, sin)
            turned = turned.astype(jnp.bfloat16)
            for j in range(CPR):
                q_out[h * CPR + j, g * RPC : (g + 1) * RPC, :] = turned[j * RPC : (j + 1) * RPC]


def drift_kernel(
    total_spans, place, span_lists, places_col, fresh_k, fresh_v, got, drift, kbuf, vbuf, sems
):
    copies = []
    for j in range(CPR):
        for which, buf in enumerate((kbuf, vbuf)):
            copy = pltpu.make_async_copy(
                got.at[:, place[0, j], place[1, j], which], buf.at[j], sems.at[which, j]
            )
            copy.start()
            copies.append(copy)
    width = fresh_k.shape[1]
    dest = lax.broadcasted_iota(jnp.int32, drift.shape, 0)
    lane = lax.broadcasted_iota(jnp.int32, drift.shape, 1)
    per_dest = total_spans // drift.shape[0]
    token = lax.broadcasted_iota(jnp.int32, (RPC, CL), 1)
    total = jnp.zeros(drift.shape, jnp.float32)
    for j in range(CPR):
        rows = slice(j * RPC, (j + 1) * RPC)
        take = (token + j * CL == places_col[rows, :]).astype(jnp.float32)
        take = take.astype(jnp.bfloat16)
        gap = jnp.zeros((RPC, width), jnp.float32)
        copies[2 * j].wait()
        copies[2 * j + 1].wait()
        for buf, fresh in ((kbuf, fresh_k), (vbuf, fresh_v)):
            cached = jnp.dot(take, buf[j].reshape(CL, width), preferred_element_type=jnp.float32)
            delta = fresh[rows, :].astype(jnp.float32) - cached
            gap = gap + delta * delta
        share = jnp.sum(gap) * (1.0 / (2.0 * KVH * HD * RPC))
        chosen = span_lists[0, j]
        total = total + jnp.where(
            (dest == chosen // per_dest) & (lane == chosen % per_dest), share, 0.0
        )
    drift[...] = total


def attend_kernel(
    heads_kv,
    group,
    place,
    places_row,
    places_col,
    q,
    new_pair,
    cos_span,
    sin_span,
    cos_token,
    sin_token,
    got,
    out,
    raw,
    keys,
    vals,
    seen,
    put,
    stay,
    cosine,
    sine,
    scores,
    sems,
):
    def loads(h, slot):
        cols = pl.ds(pl.multiple_of(h * HD, HD), HD)
        return [
            pltpu.make_async_copy(
                got.at[:, place[0, j], place[1, j], which, :, cols],
                raw.at[slot, which, j],
                sems.at[slot],
            )
            for which in range(2)
            for j in range(CPR)
        ]

    for load in loads(0, 0):
        load.start()
    block = group * RPC
    token_lane = lax.broadcasted_iota(jnp.int32, (RPC, CL), 1)
    token_row = lax.broadcasted_iota(jnp.int32, (CL, RPC), 0)
    ones = jnp.ones((RPC, HD), jnp.bfloat16)
    for j in range(CPR):
        rows = slice(j * RPC, (j + 1) * RPC)
        span = slice(j * CL, (j + 1) * CL)
        seen[j] = jnp.where(token_lane + j * CL <= places_col[rows, :], 0.0, -1e30)
        hits = (token_row + j * CL == places_row[j : j + 1, :]).astype(jnp.float32)
        hits = hits.astype(jnp.bfloat16)
        put[j] = hits
        stay[span, :] = 1.0 - jnp.dot(hits, ones, preferred_element_type=jnp.float32)
        ca, sa = cos_span[j : j + 1, :], sin_span[j : j + 1, :]
        cb, sb = cos_token[...], sin_token[...]
        cosine[span, :] = ca * cb - sa * sb
        sine[span, :] = sa * cb + ca * sb

    def head(h, carry):
        slot = lax.rem(h, 2)
        pltpu.make_async_copy(raw.at[slot], raw.at[slot], sems.at[slot]).wait()

        @pl.when(h + 1 < heads_kv)
        def _():
            for load in loads(h + 1, 1 - slot):
                load.start()

        for j in range(CPR):
            rows = slice(j * RPC, (j + 1) * RPC)
            span = slice(j * CL, (j + 1) * CL)
            old = raw[slot, 0, j].reshape(CL, HD).astype(jnp.float32)
            new = jnp.dot(put[j], new_pair[h, rows, :], preferred_element_type=jnp.float32)
            old = turn(old, cosine[span, :], sine[span, :])
            keys[span, :] = (old * stay[span, :] + new[:, :HD]).astype(jnp.bfloat16)
            old = raw[slot, 1, j].reshape(CL, HD).astype(jnp.float32)
            vals[span, :] = (old * stay[span, :] + new[:, HD:]).astype(jnp.bfloat16)
        for t in range(CPR):
            later = q[pl.ds(h * CPR + t, CPR - t)].reshape((CPR - t) * block, HD)
            scores[t * block :, t * CL : (t + 1) * CL] = lax.dot_general(
                later,
                keys[t * CL : (t + 1) * CL, :],
                (((1,), (1,)), ((), ())),
                preferred_element_type=jnp.float32,
            )
        for j in range(CPR):
            extent = (j + 1) * CL
            part = scores[j * block : (j + 1) * block, :extent]
            bias = jnp.concatenate([seen[j]] * group, axis=0)
            last = part[:, j * CL :] + bias
            part = last if j == 0 else jnp.concatenate([part[:, : j * CL], last], axis=1)
            row_max = jnp.max(part, axis=1, keepdims=True)
            weights = jnp.exp2((part - row_max) * SCALE_LOG2E)
            row_sum = jnp.sum(weights, axis=1, keepdims=True)
            mixed = jnp.dot(
                weights.astype(jnp.bfloat16),
                vals[:extent, :],
                preferred_element_type=jnp.float32,
            )
            mixed = (mixed / row_sum).astype(jnp.bfloat16)
            for g in range(group):
                start = pl.multiple_of((h * group + g) * HD, HD)
                out[j * RPC : (j + 1) * RPC, pl.ds(start, HD)] = mixed[g * RPC : (g + 1) * RPC]
        return carry

    lax.fori_loop(0, heads_kv, head, 0)


SMEM = pl.BlockSpec(memory_space=pltpu.SMEM)
VMEM = pl.BlockSpec(memory_space=pltpu.VMEM)
ANY = pl.BlockSpec(memory_space=pl.ANY)


def local(span_keys, span_values, span_row, span_lists, recompute_pos, fresh_q, fresh_k, fresh_v):
    n_store = lax.axis_size("store")
    n_req = lax.axis_size("req")
    n_tp = lax.axis_size("tp")
    n_all = n_store * n_req * n_tp
    peers = n_store * n_req
    shard_rows, tok_dev, width = span_keys.shape
    heads_kv = width // HD
    heads_q = fresh_q.shape[2] // HD
    group = heads_q // heads_kv
    bf16 = jnp.bfloat16

    def params(mebibytes):
        return pltpu.CompilerParams(vmem_limit_bytes=mebibytes << 20)


    assert n_req == BLOCKS and shard_rows * n_req == span_row.shape[0]
    plan, place = pl.pallas_call(
        functools.partial(ask_kernel, shard_rows),
        out_shape=(
            jax.ShapeDtypeStruct((peers, LANES), jnp.int32),
            jax.ShapeDtypeStruct((2, CPR), jnp.int32),
        ),
        in_specs=[SMEM, SMEM],
        out_specs=(VMEM, SMEM),
        name="ask",
    )(span_row, span_lists)
    plans = lax.all_to_all(plan, ("store", "req"), split_axis=0, concat_axis=0, tiled=True)
    piece = (2, tok_dev, width)
    climb = [(k, (k + 1) % n_req) for k in range(n_req)]
    sink = [(k, (k - 1) % n_req) for k in range(n_req)]

    def gather(size, plans, span_keys, span_values):
        moves = jax.ShapeDtypeStruct((size, tok_dev, width), bf16)
        move = pl.pallas_call(
            functools.partial(move_kernel, size),
            out_shape=(moves, moves),
            in_specs=[SMEM, ANY],
            out_specs=(ANY, ANY),
            scratch_shapes=[
                pltpu.VMEM((shard_rows, tok_dev, width), bf16),
                pltpu.VMEM((size + SLOTS, tok_dev, width), bf16),
                pltpu.VMEM((size + SLOTS, tok_dev, width), bf16),
                pltpu.SemaphoreType.DMA((2,)),
            ],
            compiler_params=params(60),
            name="move",
        )
        came = []
        for table in (span_keys, span_values):
            ups, downs = move(plans, table)
            came.append(lax.ppermute(ups, "req", climb))
            came.append(lax.ppermute(downs, "req", sink))
            plans, span_keys, span_values, _ = lax.optimization_barrier(
                (plans, span_keys, span_values, ups)
            )
        own = pl.pallas_call(
            own_kernel,
            out_shape=jax.ShapeDtypeStruct((peers, SLOTS) + piece, bf16),
            in_specs=[SMEM, ANY, ANY],
            out_specs=ANY,
            scratch_shapes=[
                pltpu.VMEM((2, shard_rows, tok_dev, width), bf16),
                pltpu.VMEM((peers, SLOTS) + piece, bf16),
                pltpu.SemaphoreType.DMA((2,)),
                pltpu.SemaphoreType.DMA,
            ],
            compiler_params=params(58),
            name="own",
        )(plans, span_keys, span_values)
        return pl.pallas_call(
            patch_kernel,
            out_shape=jax.ShapeDtypeStruct((peers, SLOTS) + piece, bf16),
            in_specs=[SMEM] + [VMEM] * 4 + [ANY],
            out_specs=ANY,
            scratch_shapes=[pltpu.SemaphoreType.DMA],
            input_output_aliases={5: 0},
            compiler_params=params(40),
            name="patch",
        )(plans, *came, own)

    load = jnp.max(jnp.sum(plans[:, LOADS : LOADS + 2 * BLOCKS], axis=0))
    level = sum((load > size).astype(jnp.int32) for size in SIZES)
    most = SLOTS * peers
    send = lax.switch(
        level,
        [functools.partial(gather, size) for size in SIZES + (most,)],
        plans,
        span_keys,
        span_values,
    )
    got = lax.all_to_all(send, ("store", "req"), split_axis=0, concat_axis=0, tiled=True)
    got = got.reshape((n_store, n_req, SLOTS) + piece)

    places, raw_q, raw_k, _ = lax.optimization_barrier((recompute_pos, fresh_q, fresh_k, send))
    places = places[0]
    raw_k = raw_k[0]
    new_v = fresh_v[0]
    angles = places.astype(jnp.float32)[:, None] * jnp.asarray(FREQ)[None, :]
    cosine = jnp.cos(angles)
    sine = jnp.sin(angles)
    queries, new_pair = pl.pallas_call(
        functools.partial(fresh_kernel, heads_kv, group),
        out_shape=(
            jax.ShapeDtypeStruct((heads_kv * CPR, group * RPC, HD), bf16),
            jax.ShapeDtypeStruct((heads_kv, RC, 2 * HD), bf16),
        ),
        in_specs=[VMEM] * 5,
        out_specs=(VMEM, VMEM),
        compiler_params=params(16),
        name="fresh",
    )(
        raw_q[0],
        raw_k,
        new_v,
        jnp.concatenate([cosine, cosine], axis=1),
        jnp.concatenate([-sine, sine], axis=1),
    )
    places_col = places[:, None]
    places_row = places.reshape(CPR, RPC)

    part = pl.pallas_call(
        functools.partial(drift_kernel, span_row.shape[0]),
        out_shape=jax.ShapeDtypeStruct((n_all, LANES), jnp.float32),
        in_specs=[SMEM, SMEM, VMEM, VMEM, VMEM, ANY],
        out_specs=VMEM,
        scratch_shapes=[
            pltpu.VMEM((CPR, n_store, tok_dev, width), bf16),
            pltpu.VMEM((CPR, n_store, tok_dev, width), bf16),
            pltpu.SemaphoreType.DMA((2, CPR)),
        ],
        compiler_params=params(50),
        cost_estimate=pl.CostEstimate(
            flops=4 * RC * CL * width, bytes_accessed=4 * CTX * width, transcendentals=0
        ),
        name="drift",
    )(place, span_lists, places_col, raw_k, new_v, got)
    parts = lax.all_to_all(part, ("store", "req", "tp"), split_axis=0, concat_axis=0, tiled=True)

    attended = pl.pallas_call(
        functools.partial(attend_kernel, heads_kv, group),
        out_shape=jax.ShapeDtypeStruct((RC, heads_q * HD), bf16),
        in_specs=[SMEM] + [VMEM] * 8 + [ANY],
        out_specs=VMEM,
        scratch_shapes=[
            pltpu.VMEM((2, 2, CPR, n_store, tok_dev, HD), bf16),
            pltpu.VMEM((CTX, HD), bf16),
            pltpu.VMEM((CTX, HD), bf16),
            pltpu.VMEM((CPR, RPC, CL), jnp.float32),
            pltpu.VMEM((CPR, CL, RPC), bf16),
            pltpu.VMEM((CTX, HD), jnp.float32),
            pltpu.VMEM((CTX, HD), jnp.float32),
            pltpu.VMEM((CTX, HD), jnp.float32),
            pltpu.VMEM((CPR * group * RPC, CTX), jnp.float32),
            pltpu.SemaphoreType.DMA((2,)),
        ],
        compiler_params=params(50),
        cost_estimate=pl.CostEstimate(
            flops=2 * heads_q * RC * CTX * HD * 2,
            bytes_accessed=4 * CTX * width + 4 * RC * heads_q * HD,
            transcendentals=heads_q * RC * CTX // 2,
        ),
        name="attend",
    )(
        place,
        places_row,
        places_col,
        queries,
        new_pair,
        jnp.asarray(COS_SPAN),
        jnp.asarray(SIN_SPAN),
        jnp.asarray(COS_TOKEN),
        jnp.asarray(SIN_TOKEN),
        got,
    )
    per_dest = span_row.shape[0] // n_all
    drift_part = jnp.sum(parts, axis=0)[:per_dest]
    return (attended[None], drift_part)


def solution(mesh):
    in_specs = (
        P("req", "store", "tp"),
        P("req", "store", "tp"),
        P(),
        P(("store", "req"), None),
        P(("store", "req"), None),
        P(("store", "req"), None, "tp"),
        P(("store", "req"), None, "tp"),
        P(("store", "req"), None, "tp"),
    )
    out_specs = (P(("store", "req"), None, "tp"), P(("store", "req", "tp")))
    return jax.shard_map(local, mesh=mesh, in_specs=in_specs, out_specs=out_specs, check_vma=False)
```

```python
import functools

import jax
import jax.numpy as jnp
import numpy as np
from jax import lax
from jax.experimental import pallas as pl
from jax.experimental.pallas import tpu as pltpu
from jax.sharding import PartitionSpec as P

HD = 128
HALF = HD // 2
CPR = 8
RPC = 16
CL = 256
CTX = CPR * CL
RC = CPR * RPC
KVH = 8
BLOCKS = 4
SLOTS = CPR // BLOCKS
SIZES = (22, 24, 26, 28, 30, 33, 36, 40)
KEPT, UP, DOWN, FROM_BELOW, FROM_ABOVE, LOADS = 0, 4, 8, 12, 13, 16
LANES = 128
SCALE_LOG2E = float(HD ** -0.5 * np.log2(np.e))

FREQ = np.exp(-np.log(500000.0) * np.arange(HALF) / HALF).astype(np.float32)


def angle_tables(positions):
    angles = positions[:, None].astype(np.float64) * FREQ[None, :].astype(np.float64)
    cosine = np.cos(angles).astype(np.float32)
    sine = np.sin(angles).astype(np.float32)
    return (
        np.concatenate([cosine, cosine], axis=1),
        np.concatenate([-sine, sine], axis=1),
    )


COS_SPAN, SIN_SPAN = angle_tables(CL * np.arange(CPR))
COS_TOKEN, SIN_TOKEN = angle_tables(np.arange(CL))


def turn(x, cosine, sine):
    return x * cosine + pltpu.roll(x, HALF, 1) * sine


def ask_kernel(shard_rows, span_row, span_lists, plan, place):
    spans = [span_row[span_lists[0, j]] for j in range(CPR)]
    homes = [row // shard_rows for row in spans]
    rows = [row % shard_rows for row in spans]
    one = [[jnp.where(home == k, 1, 0) for home in homes] for k in range(BLOCKS)]
    counts = [sum(one[k]) for k in range(BLOCKS)]
    sums = []
    total = jnp.int32(0)
    for k in range(BLOCKS):
        total = total + counts[k] - SLOTS
        sums.append(total)
    low, high = jnp.minimum(sums[0], sums[1]), jnp.maximum(sums[0], sums[1])
    low2, high2 = jnp.minimum(sums[2], sums[3]), jnp.maximum(sums[2], sums[3])
    middle, middle2 = jnp.maximum(low, low2), jnp.minimum(high, high2)
    first, second = jnp.minimum(middle, middle2), jnp.maximum(middle, middle2)
    whole = sums[0] + sums[1] + sums[2] + sums[3]
    mixed = lax.rem(sum(span_lists[0, j] for j in range(CPR)), 4) == 0
    level = jnp.abs(whole - BLOCKS * first) <= jnp.abs(whole - BLOCKS * second)
    shift = jnp.where(level != mixed, first, second)
    flow = [x - shift for x in sums]
    up = [jnp.maximum(x, 0) for x in flow]
    down = [jnp.maximum(-flow[k - 1], 0) for k in range(BLOCKS)]
    keep = [counts[k] - up[k] - down[k] for k in range(BLOCKS)]

    block = lax.broadcasted_iota(jnp.int32, plan.shape, 0) % BLOCKS
    lane = lax.broadcasted_iota(jnp.int32, plan.shape, 1)
    out = jnp.zeros(plan.shape, jnp.int32)
    for k in range(BLOCKS):
        own = block == k
        heads = (
            (KEPT, keep[k]),
            (UP, up[k]),
            (DOWN, down[k]),
            (FROM_BELOW, up[k - 1]),
            (FROM_ABOVE, down[(k + 1) % BLOCKS]),
        )
        for at, value in heads:
            out = jnp.where(own & (lane == at), value, out)
        out = jnp.where(lane == LOADS + k, up[k], out)
        out = jnp.where(lane == LOADS + BLOCKS + k, down[k], out)

    def of(table, k):
        value = table[0]
        for i in range(1, BLOCKS):
            value = jnp.where(k == i, table[i], value)
        return value

    base_below = [keep[k] for k in range(BLOCKS)]
    base_above = [keep[k] + up[k - 1] for k in range(BLOCKS)]
    for j in range(CPR):
        home = homes[j]
        rank = jnp.int32(0)
        for i in range(j):
            rank = rank + jnp.where(homes[i] == home, 1, 0)
        kept = of(keep, home)
        after = rank - kept
        ups = of(up, home)
        stays = after < 0
        climbs = after < ups
        at = jnp.where(
            stays, KEPT + 1 + rank, jnp.where(climbs, UP + 1 + after, DOWN + 1 + after - ups)
        )
        out = jnp.where((block == home) & (lane == at), rows[j], out)
        above = lax.rem(home + 1, BLOCKS)
        below = lax.rem(home + BLOCKS - 1, BLOCKS)
        place[0, j] = jnp.where(stays, home, jnp.where(climbs, above, below))
        place[1, j] = jnp.where(
            stays,
            rank,
            jnp.where(climbs, of(base_below, above) + after, of(base_above, below) + after - ups),
        )
    plan[...] = out


def level_kernel(plan, out):
    lane = lax.broadcasted_iota(jnp.int32, (1, LANES), 1)
    loads = jnp.sum(plan[...].astype(jnp.float32), axis=0, keepdims=True)
    loads = jnp.where((lane >= LOADS) & (lane < LOADS + 2 * BLOCKS), loads, 0.0)
    load = jnp.max(loads).astype(jnp.int32)
    level = jnp.int32(0)
    for size in SIZES:
        level = level + jnp.where(load > size, 1, 0)
    out[0] = level


def move_kernel(size, plan, table, up_out, down_out, rows, up_stage, down_stage, sems):
    load = pltpu.make_async_copy(table, rows, sems.at[0])
    load.start()
    load.wait()

    def fill(r, marks):
        ends = []
        for at, stage, mark in ((UP, up_stage, marks[0]), (DOWN, down_stage, marks[1])):
            for i in range(SLOTS):
                stage[mark + i] = rows[plan[r, at + 1 + i]]
            ends.append(mark + plan[r, at])
        return tuple(ends)

    lax.fori_loop(0, plan.shape[0], fill, (jnp.int32(0), jnp.int32(0)), unroll=4)
    stores = [
        pltpu.make_async_copy(stage.at[pl.ds(0, size)], out, sems.at[i])
        for i, (stage, out) in enumerate(((up_stage, up_out), (down_stage, down_out)))
    ]
    for store in stores:
        store.start()
    for store in stores:
        store.wait()


def own_kernel(plan, keys, values, send, pool, stage, sems, out_sem):
    loads = [
        pltpu.make_async_copy(table, pool.at[i], sems.at[i])
        for i, table in enumerate((keys, values))
    ]
    for load in loads:
        load.start()
    for load in loads:
        load.wait()

    def fill(r, carry):
        for t in range(SLOTS):
            row = plan[r, KEPT + 1 + t]
            stage[r, t, 0] = pool[0, row]
            stage[r, t, 1] = pool[1, row]
        pltpu.make_async_copy(stage.at[r], send.at[r], out_sem).start()
        return carry

    lax.fori_loop(0, send.shape[0], fill, 0, unroll=4)
    pltpu.make_async_copy(stage, send, out_sem).wait()


def patch_kernel(plan, below_k, above_k, below_v, above_v, own, send, sem):
    def fill(r, marks):
        kept = plan[r, KEPT]
        second = kept + plan[r, FROM_BELOW]
        for t in range(SLOTS):

            @pl.when((t >= kept) & (t < second))
            def _():
                row = marks[0] + t - kept
                pltpu.make_async_copy(below_k.at[row], send.at[r, t, 0], sem).start()
                pltpu.make_async_copy(below_v.at[row], send.at[r, t, 1], sem).start()

            @pl.when(t >= second)
            def _():
                row = marks[1] + t - second
                pltpu.make_async_copy(above_k.at[row], send.at[r, t, 0], sem).start()
                pltpu.make_async_copy(above_v.at[row], send.at[r, t, 1], sem).start()

        return marks[0] + plan[r, FROM_BELOW], marks[1] + plan[r, FROM_ABOVE]

    ends = lax.fori_loop(0, send.shape[0], fill, (jnp.int32(0), jnp.int32(0)), unroll=4)

    def drain(i, carry):
        pltpu.make_async_copy(send.at[0, 0], send.at[0, 0], sem).wait()
        return carry

    lax.fori_loop(0, ends[0] + ends[1], drain, 0)


def fresh_kernel(heads_kv, group, q, k, v, cosine, sine, q_out, pair_out):
    cos = cosine[...]
    sin = sine[...]
    for h in range(heads_kv):
        cols = slice(h * HD, (h + 1) * HD)
        turned = turn(k[:, cols].astype(jnp.float32), cos, sin)
        pair_out[h, :, :HD] = turned.astype(jnp.bfloat16)
        pair_out[h, :, HD:] = v[:, cols]
        for g in range(group):
            n = h * group + g
            turned = turn(q[:, n * HD : (n + 1) * HD].astype(jnp.float32), cos, sin)
            turned = turned.astype(jnp.bfloat16)
            for j in range(CPR):
                q_out[h * CPR + j, g * RPC : (g + 1) * RPC, :] = turned[j * RPC : (j + 1) * RPC]


def drift_kernel(
    total_spans, place, span_lists, places_col, fresh_k, fresh_v, got, drift, kbuf, vbuf, sems
):
    copies = []
    for j in range(CPR):
        for which, buf in enumerate((kbuf, vbuf)):
            copy = pltpu.make_async_copy(
                got.at[:, place[0, j], place[1, j], which], buf.at[j], sems.at[which, j]
            )
            copy.start()
            copies.append(copy)
    width = fresh_k.shape[1]
    dest = lax.broadcasted_iota(jnp.int32, drift.shape, 0)
    lane = lax.broadcasted_iota(jnp.int32, drift.shape, 1)
    per_dest = total_spans // drift.shape[0]
    token = lax.broadcasted_iota(jnp.int32, (RPC, CL), 1)
    total = jnp.zeros(drift.shape, jnp.float32)
    for j in range(CPR):
        rows = slice(j * RPC, (j + 1) * RPC)
        take = (token + j * CL == places_col[rows, :]).astype(jnp.float32)
        take = take.astype(jnp.bfloat16)
        gap = jnp.zeros((RPC, width), jnp.float32)
        copies[2 * j].wait()
        copies[2 * j + 1].wait()
        for buf, fresh in ((kbuf, fresh_k), (vbuf, fresh_v)):
            cached = jnp.dot(take, buf[j].reshape(CL, width), preferred_element_type=jnp.float32)
            delta = fresh[rows, :].astype(jnp.float32) - cached
            gap = gap + delta * delta
        share = jnp.sum(gap) * (1.0 / (2.0 * KVH * HD * RPC))
        chosen = span_lists[0, j]
        total = total + jnp.where(
            (dest == chosen // per_dest) & (lane == chosen % per_dest), share, 0.0
        )
    drift[...] = total


def attend_kernel(
    heads_kv,
    group,
    place,
    places_row,
    places_col,
    q,
    new_pair,
    cos_span,
    sin_span,
    cos_token,
    sin_token,
    got,
    out,
    raw,
    keys,
    vals,
    seen,
    put,
    stay,
    cosine,
    sine,
    scores,
    sems,
):
    def loads(h, slot):
        cols = pl.ds(pl.multiple_of(h * HD, HD), HD)
        return [
            pltpu.make_async_copy(
                got.at[:, place[0, j], place[1, j], which, :, cols],
                raw.at[slot, which, j],
                sems.at[slot],
            )
            for which in range(2)
            for j in range(CPR)
        ]

    for load in loads(0, 0):
        load.start()
    block = group * RPC
    token_lane = lax.broadcasted_iota(jnp.int32, (RPC, CL), 1)
    token_row = lax.broadcasted_iota(jnp.int32, (CL, RPC), 0)
    ones = jnp.ones((RPC, HD), jnp.bfloat16)
    for j in range(CPR):
        rows = slice(j * RPC, (j + 1) * RPC)
        span = slice(j * CL, (j + 1) * CL)
        seen[j] = jnp.where(token_lane + j * CL <= places_col[rows, :], 0.0, -1e30)
        hits = (token_row + j * CL == places_row[j : j + 1, :]).astype(jnp.float32)
        hits = hits.astype(jnp.bfloat16)
        put[j] = hits
        stay[span, :] = 1.0 - jnp.dot(hits, ones, preferred_element_type=jnp.float32)
        ca, sa = cos_span[j : j + 1, :], sin_span[j : j + 1, :]
        cb, sb = cos_token[...], sin_token[...]
        cosine[span, :] = ca * cb - sa * sb
        sine[span, :] = sa * cb + ca * sb

    def head(h, carry):
        slot = lax.rem(h, 2)
        pltpu.make_async_copy(raw.at[slot], raw.at[slot], sems.at[slot]).wait()

        @pl.when(h + 1 < heads_kv)
        def _():
            for load in loads(h + 1, 1 - slot):
                load.start()

        for j in range(CPR):
            rows = slice(j * RPC, (j + 1) * RPC)
            span = slice(j * CL, (j + 1) * CL)
            old = raw[slot, 0, j].reshape(CL, HD).astype(jnp.float32)
            new = jnp.dot(put[j], new_pair[h, rows, :], preferred_element_type=jnp.float32)
            old = turn(old, cosine[span, :], sine[span, :])
            keys[span, :] = (old * stay[span, :] + new[:, :HD]).astype(jnp.bfloat16)
            old = raw[slot, 1, j].reshape(CL, HD).astype(jnp.float32)
            vals[span, :] = (old * stay[span, :] + new[:, HD:]).astype(jnp.bfloat16)
        for t in range(CPR):
            later = q[pl.ds(h * CPR + t, CPR - t)].reshape((CPR - t) * block, HD)
            scores[t * block :, t * CL : (t + 1) * CL] = lax.dot_general(
                later,
                keys[t * CL : (t + 1) * CL, :],
                (((1,), (1,)), ((), ())),
                preferred_element_type=jnp.float32,
            )
        for j in range(CPR):
            extent = (j + 1) * CL
            part = scores[j * block : (j + 1) * block, :extent]
            bias = jnp.concatenate([seen[j]] * group, axis=0)
            last = part[:, j * CL :] + bias
            part = last if j == 0 else jnp.concatenate([part[:, : j * CL], last], axis=1)
            row_max = jnp.max(part, axis=1, keepdims=True)
            weights = jnp.exp2((part - row_max) * SCALE_LOG2E)
            row_sum = jnp.sum(weights, axis=1, keepdims=True)
            mixed = jnp.dot(
                weights.astype(jnp.bfloat16),
                vals[:extent, :],
                preferred_element_type=jnp.float32,
            )
            mixed = (mixed / row_sum).astype(jnp.bfloat16)
            for g in range(group):
                start = pl.multiple_of((h * group + g) * HD, HD)
                out[j * RPC : (j + 1) * RPC, pl.ds(start, HD)] = mixed[g * RPC : (g + 1) * RPC]
        return carry

    lax.fori_loop(0, heads_kv, head, 0)


SMEM = pl.BlockSpec(memory_space=pltpu.SMEM)
VMEM = pl.BlockSpec(memory_space=pltpu.VMEM)
ANY = pl.BlockSpec(memory_space=pl.ANY)


def local(span_keys, span_values, span_row, span_lists, recompute_pos, fresh_q, fresh_k, fresh_v):
    n_store = lax.axis_size("store")
    n_req = lax.axis_size("req")
    n_tp = lax.axis_size("tp")
    n_all = n_store * n_req * n_tp
    peers = n_store * n_req
    shard_rows, tok_dev, width = span_keys.shape
    heads_kv = width // HD
    heads_q = fresh_q.shape[2] // HD
    group = heads_q // heads_kv
    bf16 = jnp.bfloat16

    def params(mebibytes):
        return pltpu.CompilerParams(vmem_limit_bytes=mebibytes << 20)


    assert n_req == BLOCKS and shard_rows * n_req == span_row.shape[0]
    plan, place = pl.pallas_call(
        functools.partial(ask_kernel, shard_rows),
        out_shape=(
            jax.ShapeDtypeStruct((peers, LANES), jnp.int32),
            jax.ShapeDtypeStruct((2, CPR), jnp.int32),
        ),
        in_specs=[SMEM, SMEM],
        out_specs=(VMEM, SMEM),
        name="ask",
    )(span_row, span_lists)
    plans = lax.all_to_all(plan, ("store", "req"), split_axis=0, concat_axis=0, tiled=True)
    piece = (2, tok_dev, width)
    climb = [(k, (k + 1) % n_req) for k in range(n_req)]
    sink = [(k, (k - 1) % n_req) for k in range(n_req)]

    def gather(size, plans, span_keys, span_values):
        moves = jax.ShapeDtypeStruct((size, tok_dev, width), bf16)
        move = pl.pallas_call(
            functools.partial(move_kernel, size),
            out_shape=(moves, moves),
            in_specs=[SMEM, ANY],
            out_specs=(ANY, ANY),
            scratch_shapes=[
                pltpu.VMEM((shard_rows, tok_dev, width), bf16),
                pltpu.VMEM((size + SLOTS, tok_dev, width), bf16),
                pltpu.VMEM((size + SLOTS, tok_dev, width), bf16),
                pltpu.SemaphoreType.DMA((2,)),
            ],
            compiler_params=params(60),
            name="move",
        )
        came = []
        for table in (span_keys, span_values):
            ups, downs = move(plans, table)
            came.append(lax.ppermute(ups, "req", climb))
            came.append(lax.ppermute(downs, "req", sink))
            plans, span_keys, span_values, _ = lax.optimization_barrier(
                (plans, span_keys, span_values, ups)
            )
        own = pl.pallas_call(
            own_kernel,
            out_shape=jax.ShapeDtypeStruct((peers, SLOTS) + piece, bf16),
            in_specs=[SMEM, ANY, ANY],
            out_specs=ANY,
            scratch_shapes=[
                pltpu.VMEM((2, shard_rows, tok_dev, width), bf16),
                pltpu.VMEM((peers, SLOTS) + piece, bf16),
                pltpu.SemaphoreType.DMA((2,)),
                pltpu.SemaphoreType.DMA,
            ],
            compiler_params=params(58),
            name="own",
        )(plans, span_keys, span_values)
        return pl.pallas_call(
            patch_kernel,
            out_shape=jax.ShapeDtypeStruct((peers, SLOTS) + piece, bf16),
            in_specs=[SMEM] + [VMEM] * 4 + [ANY],
            out_specs=ANY,
            scratch_shapes=[pltpu.SemaphoreType.DMA],
            input_output_aliases={5: 0},
            compiler_params=params(40),
            name="patch",
        )(plans, *came, own)

    level = pl.pallas_call(
        level_kernel,
        out_shape=jax.ShapeDtypeStruct((1,), jnp.int32),
        in_specs=[VMEM],
        out_specs=SMEM,
        name="level",
    )(plans)[0]
    most = SLOTS * peers
    send = lax.switch(
        level,
        [functools.partial(gather, size) for size in SIZES + (most,)],
        plans,
        span_keys,
        span_values,
    )
    got = lax.all_to_all(send, ("store", "req"), split_axis=0, concat_axis=0, tiled=True)
    got = got.reshape((n_store, n_req, SLOTS) + piece)

    places, raw_q, raw_k, _ = lax.optimization_barrier((recompute_pos, fresh_q, fresh_k, send))
    places = places[0]
    raw_k = raw_k[0]
    new_v = fresh_v[0]
    angles = places.astype(jnp.float32)[:, None] * jnp.asarray(FREQ)[None, :]
    cosine = jnp.cos(angles)
    sine = jnp.sin(angles)
    queries, new_pair = pl.pallas_call(
        functools.partial(fresh_kernel, heads_kv, group),
        out_shape=(
            jax.ShapeDtypeStruct((heads_kv * CPR, group * RPC, HD), bf16),
            jax.ShapeDtypeStruct((heads_kv, RC, 2 * HD), bf16),
        ),
        in_specs=[VMEM] * 5,
        out_specs=(VMEM, VMEM),
        compiler_params=params(16),
        name="fresh",
    )(
        raw_q[0],
        raw_k,
        new_v,
        jnp.concatenate([cosine, cosine], axis=1),
        jnp.concatenate([-sine, sine], axis=1),
    )
    places_col = places[:, None]
    places_row = places.reshape(CPR, RPC)

    part = pl.pallas_call(
        functools.partial(drift_kernel, span_row.shape[0]),
        out_shape=jax.ShapeDtypeStruct((n_all, LANES), jnp.float32),
        in_specs=[SMEM, SMEM, VMEM, VMEM, VMEM, ANY],
        out_specs=VMEM,
        scratch_shapes=[
            pltpu.VMEM((CPR, n_store, tok_dev, width), bf16),
            pltpu.VMEM((CPR, n_store, tok_dev, width), bf16),
            pltpu.SemaphoreType.DMA((2, CPR)),
        ],
        compiler_params=params(50),
        cost_estimate=pl.CostEstimate(
            flops=4 * RC * CL * width, bytes_accessed=4 * CTX * width, transcendentals=0
        ),
        name="drift",
    )(place, span_lists, places_col, raw_k, new_v, got)
    parts = lax.all_to_all(part, ("store", "req", "tp"), split_axis=0, concat_axis=0, tiled=True)

    attended = pl.pallas_call(
        functools.partial(attend_kernel, heads_kv, group),
        out_shape=jax.ShapeDtypeStruct((RC, heads_q * HD), bf16),
        in_specs=[SMEM] + [VMEM] * 8 + [ANY],
        out_specs=VMEM,
        scratch_shapes=[
            pltpu.VMEM((2, 2, CPR, n_store, tok_dev, HD), bf16),
            pltpu.VMEM((CTX, HD), bf16),
            pltpu.VMEM((CTX, HD), bf16),
            pltpu.VMEM((CPR, RPC, CL), jnp.float32),
            pltpu.VMEM((CPR, CL, RPC), bf16),
            pltpu.VMEM((CTX, HD), jnp.float32),
            pltpu.VMEM((CTX, HD), jnp.float32),
            pltpu.VMEM((CTX, HD), jnp.float32),
            pltpu.VMEM((CPR * group * RPC, CTX), jnp.float32),
            pltpu.SemaphoreType.DMA((2,)),
        ],
        compiler_params=params(50),
        cost_estimate=pl.CostEstimate(
            flops=2 * heads_q * RC * CTX * HD * 2,
            bytes_accessed=4 * CTX * width + 4 * RC * heads_q * HD,
            transcendentals=heads_q * RC * CTX // 2,
        ),
        name="attend",
    )(
        place,
        places_row,
        places_col,
        queries,
        new_pair,
        jnp.asarray(COS_SPAN),
        jnp.asarray(SIN_SPAN),
        jnp.asarray(COS_TOKEN),
        jnp.asarray(SIN_TOKEN),
        got,
    )
    per_dest = span_row.shape[0] // n_all
    drift_part = jnp.sum(parts, axis=0)[:per_dest]
    return (attended[None], drift_part)


def solution(mesh):
    in_specs = (
        P("req", "store", "tp"),
        P("req", "store", "tp"),
        P(),
        P(("store", "req"), None),
        P(("store", "req"), None),
        P(("store", "req"), None, "tp"),
        P(("store", "req"), None, "tp"),
        P(("store", "req"), None, "tp"),
    )
    out_specs = (P(("store", "req"), None, "tp"), P(("store", "req", "tp")))
    return jax.shard_map(local, mesh=mesh, in_specs=in_specs, out_specs=out_specs, check_vma=False)
```

```python
import functools

import jax
import jax.numpy as jnp
import numpy as np
from jax import lax
from jax.experimental import pallas as pl
from jax.experimental.pallas import tpu as pltpu
from jax.sharding import PartitionSpec as P

HD = 128
HALF = HD // 2
CPR = 8
RPC = 16
CL = 256
CTX = CPR * CL
RC = CPR * RPC
KVH = 8
BLOCKS = 4
SLOTS = CPR // BLOCKS
SIZES = (22, 24, 26, 28, 30, 33, 36, 40)
KEPT, UP, DOWN, FROM_BELOW, FROM_ABOVE, LOADS = 0, 4, 8, 12, 13, 16
LANES = 128
SCALE_LOG2E = float(HD ** -0.5 * np.log2(np.e))

FREQ = np.exp(-np.log(500000.0) * np.arange(HALF) / HALF).astype(np.float32)


def angle_tables(positions):
    angles = positions[:, None].astype(np.float64) * FREQ[None, :].astype(np.float64)
    cosine = np.cos(angles).astype(np.float32)
    sine = np.sin(angles).astype(np.float32)
    return (
        np.concatenate([cosine, cosine], axis=1),
        np.concatenate([-sine, sine], axis=1),
    )


COS_SPAN, SIN_SPAN = angle_tables(CL * np.arange(CPR))
COS_TOKEN, SIN_TOKEN = angle_tables(np.arange(CL))


def turn(x, cosine, sine):
    return x * cosine + pltpu.roll(x, HALF, 1) * sine


def ask_kernel(shard_rows, span_row, span_lists, plan, place):
    spans = [span_row[span_lists[0, j]] for j in range(CPR)]
    homes = [row // shard_rows for row in spans]
    rows = [row % shard_rows for row in spans]
    one = [[jnp.where(home == k, 1, 0) for home in homes] for k in range(BLOCKS)]
    counts = [sum(one[k]) for k in range(BLOCKS)]
    sums = []
    total = jnp.int32(0)
    for k in range(BLOCKS):
        total = total + counts[k] - SLOTS
        sums.append(total)
    low, high = jnp.minimum(sums[0], sums[1]), jnp.maximum(sums[0], sums[1])
    low2, high2 = jnp.minimum(sums[2], sums[3]), jnp.maximum(sums[2], sums[3])
    middle, middle2 = jnp.maximum(low, low2), jnp.minimum(high, high2)
    first, second = jnp.minimum(middle, middle2), jnp.maximum(middle, middle2)
    whole = sums[0] + sums[1] + sums[2] + sums[3]
    mixed = lax.rem(sum(span_lists[0, j] for j in range(CPR)), 4) == 0
    level = jnp.abs(whole - BLOCKS * first) <= jnp.abs(whole - BLOCKS * second)
    shift = jnp.where(level != mixed, first, second)
    flow = [x - shift for x in sums]
    up = [jnp.maximum(x, 0) for x in flow]
    down = [jnp.maximum(-flow[k - 1], 0) for k in range(BLOCKS)]
    keep = [counts[k] - up[k] - down[k] for k in range(BLOCKS)]

    block = lax.broadcasted_iota(jnp.int32, plan.shape, 0) % BLOCKS
    lane = lax.broadcasted_iota(jnp.int32, plan.shape, 1)
    out = jnp.zeros(plan.shape, jnp.int32)
    for k in range(BLOCKS):
        own = block == k
        heads = (
            (KEPT, keep[k]),
            (UP, up[k]),
            (DOWN, down[k]),
            (FROM_BELOW, up[k - 1]),
            (FROM_ABOVE, down[(k + 1) % BLOCKS]),
        )
        for at, value in heads:
            out = jnp.where(own & (lane == at), value, out)
        out = jnp.where(lane == LOADS + k, up[k], out)
        out = jnp.where(lane == LOADS + BLOCKS + k, down[k], out)

    def of(table, k):
        value = table[0]
        for i in range(1, BLOCKS):
            value = jnp.where(k == i, table[i], value)
        return value

    base_below = [keep[k] for k in range(BLOCKS)]
    base_above = [keep[k] + up[k - 1] for k in range(BLOCKS)]
    for j in range(CPR):
        home = homes[j]
        rank = jnp.int32(0)
        for i in range(j):
            rank = rank + jnp.where(homes[i] == home, 1, 0)
        kept = of(keep, home)
        after = rank - kept
        ups = of(up, home)
        stays = after < 0
        climbs = after < ups
        at = jnp.where(
            stays, KEPT + 1 + rank, jnp.where(climbs, UP + 1 + after, DOWN + 1 + after - ups)
        )
        out = jnp.where((block == home) & (lane == at), rows[j], out)
        above = lax.rem(home + 1, BLOCKS)
        below = lax.rem(home + BLOCKS - 1, BLOCKS)
        place[0, j] = jnp.where(stays, home, jnp.where(climbs, above, below))
        place[1, j] = jnp.where(
            stays,
            rank,
            jnp.where(climbs, of(base_below, above) + after, of(base_above, below) + after - ups),
        )
    plan[...] = out


def level_kernel(plan, out):
    lane = lax.broadcasted_iota(jnp.int32, (1, LANES), 1)
    loads = jnp.sum(plan[...].astype(jnp.float32), axis=0, keepdims=True)
    loads = jnp.where((lane >= LOADS) & (lane < LOADS + 2 * BLOCKS), loads, 0.0)
    load = jnp.max(loads).astype(jnp.int32)
    level = jnp.int32(0)
    for size in SIZES:
        level = level + jnp.where(load > size, 1, 0)
    out[0] = level


def move_kernel(size, plans, table, up_out, down_out, plan, rows, up_stage, down_stage, sems):
    loads = [
        pltpu.make_async_copy(plans, plan, sems.at[0]),
        pltpu.make_async_copy(table, rows, sems.at[1]),
    ]
    for load in loads:
        load.start()
    for load in loads:
        load.wait()

    def fill(r, marks):
        ends = []
        for at, stage, mark in ((UP, up_stage, marks[0]), (DOWN, down_stage, marks[1])):
            for i in range(SLOTS):
                stage[mark + i] = rows[plan[r, at + 1 + i]]
            ends.append(mark + plan[r, at])
        return tuple(ends)

    lax.fori_loop(0, plan.shape[0], fill, (jnp.int32(0), jnp.int32(0)), unroll=4)
    stores = [
        pltpu.make_async_copy(stage.at[pl.ds(0, size)], out, sems.at[i])
        for i, (stage, out) in enumerate(((up_stage, up_out), (down_stage, down_out)))
    ]
    for store in stores:
        store.start()
    for store in stores:
        store.wait()


def own_kernel(plan, keys, values, send, pool, stage, sems, out_sem):
    loads = [
        pltpu.make_async_copy(table, pool.at[i], sems.at[i])
        for i, table in enumerate((keys, values))
    ]
    for load in loads:
        load.start()
    for load in loads:
        load.wait()

    def fill(r, carry):
        for t in range(SLOTS):
            row = plan[r, KEPT + 1 + t]
            stage[r, t, 0] = pool[0, row]
            stage[r, t, 1] = pool[1, row]
        pltpu.make_async_copy(stage.at[r], send.at[r], out_sem).start()
        return carry

    lax.fori_loop(0, send.shape[0], fill, 0, unroll=4)
    pltpu.make_async_copy(stage, send, out_sem).wait()


def patch_kernel(plan, below_k, above_k, below_v, above_v, own, send, sem):
    def fill(r, marks):
        kept = plan[r, KEPT]
        second = kept + plan[r, FROM_BELOW]
        for t in range(SLOTS):

            @pl.when((t >= kept) & (t < second))
            def _():
                row = marks[0] + t - kept
                pltpu.make_async_copy(below_k.at[row], send.at[r, t, 0], sem).start()
                pltpu.make_async_copy(below_v.at[row], send.at[r, t, 1], sem).start()

            @pl.when(t >= second)
            def _():
                row = marks[1] + t - second
                pltpu.make_async_copy(above_k.at[row], send.at[r, t, 0], sem).start()
                pltpu.make_async_copy(above_v.at[row], send.at[r, t, 1], sem).start()

        return marks[0] + plan[r, FROM_BELOW], marks[1] + plan[r, FROM_ABOVE]

    ends = lax.fori_loop(0, send.shape[0], fill, (jnp.int32(0), jnp.int32(0)), unroll=4)

    def drain(i, carry):
        pltpu.make_async_copy(send.at[0, 0], send.at[0, 0], sem).wait()
        return carry

    lax.fori_loop(0, ends[0] + ends[1], drain, 0)


def fresh_kernel(heads_kv, group, q, k, v, cosine, sine, q_out, pair_out):
    cos = cosine[...]
    sin = sine[...]
    for h in range(heads_kv):
        cols = slice(h * HD, (h + 1) * HD)
        turned = turn(k[:, cols].astype(jnp.float32), cos, sin)
        pair_out[h, :, :HD] = turned.astype(jnp.bfloat16)
        pair_out[h, :, HD:] = v[:, cols]
        for g in range(group):
            n = h * group + g
            turned = turn(q[:, n * HD : (n + 1) * HD].astype(jnp.float32), cos, sin)
            turned = turned.astype(jnp.bfloat16)
            for j in range(CPR):
                q_out[h * CPR + j, g * RPC : (g + 1) * RPC, :] = turned[j * RPC : (j + 1) * RPC]


def drift_kernel(
    total_spans, place, span_lists, places_col, fresh_k, fresh_v, got, drift, kbuf, vbuf, sems
):
    copies = []
    for j in range(CPR):
        for which, buf in enumerate((kbuf, vbuf)):
            copy = pltpu.make_async_copy(
                got.at[:, place[0, j], place[1, j], which], buf.at[j], sems.at[which, j]
            )
            copy.start()
            copies.append(copy)
    width = fresh_k.shape[1]
    dest = lax.broadcasted_iota(jnp.int32, drift.shape, 0)
    lane = lax.broadcasted_iota(jnp.int32, drift.shape, 1)
    per_dest = total_spans // drift.shape[0]
    token = lax.broadcasted_iota(jnp.int32, (RPC, CL), 1)
    total = jnp.zeros(drift.shape, jnp.float32)
    for j in range(CPR):
        rows = slice(j * RPC, (j + 1) * RPC)
        take = (token + j * CL == places_col[rows, :]).astype(jnp.float32)
        take = take.astype(jnp.bfloat16)
        gap = jnp.zeros((RPC, width), jnp.float32)
        copies[2 * j].wait()
        copies[2 * j + 1].wait()
        for buf, fresh in ((kbuf, fresh_k), (vbuf, fresh_v)):
            cached = jnp.dot(take, buf[j].reshape(CL, width), preferred_element_type=jnp.float32)
            delta = fresh[rows, :].astype(jnp.float32) - cached
            gap = gap + delta * delta
        share = jnp.sum(gap) * (1.0 / (2.0 * KVH * HD * RPC))
        chosen = span_lists[0, j]
        total = total + jnp.where(
            (dest == chosen // per_dest) & (lane == chosen % per_dest), share, 0.0
        )
    drift[...] = total


def attend_kernel(
    heads_kv,
    group,
    place,
    places_row,
    places_col,
    q,
    new_pair,
    cos_span,
    sin_span,
    cos_token,
    sin_token,
    got,
    out,
    raw,
    keys,
    vals,
    seen,
    put,
    stay,
    cosine,
    sine,
    scores,
    sems,
):
    def loads(h, slot):
        cols = pl.ds(pl.multiple_of(h * HD, HD), HD)
        return [
            pltpu.make_async_copy(
                got.at[:, place[0, j], place[1, j], which, :, cols],
                raw.at[slot, which, j],
                sems.at[slot],
            )
            for which in range(2)
            for j in range(CPR)
        ]

    for load in loads(0, 0):
        load.start()
    block = group * RPC
    token_lane = lax.broadcasted_iota(jnp.int32, (RPC, CL), 1)
    token_row = lax.broadcasted_iota(jnp.int32, (CL, RPC), 0)
    ones = jnp.ones((RPC, HD), jnp.bfloat16)
    for j in range(CPR):
        rows = slice(j * RPC, (j + 1) * RPC)
        span = slice(j * CL, (j + 1) * CL)
        seen[j] = jnp.where(token_lane + j * CL <= places_col[rows, :], 0.0, -1e30)
        hits = (token_row + j * CL == places_row[j : j + 1, :]).astype(jnp.float32)
        hits = hits.astype(jnp.bfloat16)
        put[j] = hits
        stay[span, :] = 1.0 - jnp.dot(hits, ones, preferred_element_type=jnp.float32)
        ca, sa = cos_span[j : j + 1, :], sin_span[j : j + 1, :]
        cb, sb = cos_token[...], sin_token[...]
        cosine[span, :] = ca * cb - sa * sb
        sine[span, :] = sa * cb + ca * sb

    def head(h, carry):
        slot = lax.rem(h, 2)
        pltpu.make_async_copy(raw.at[slot], raw.at[slot], sems.at[slot]).wait()

        @pl.when(h + 1 < heads_kv)
        def _():
            for load in loads(h + 1, 1 - slot):
                load.start()

        for j in range(CPR):
            rows = slice(j * RPC, (j + 1) * RPC)
            span = slice(j * CL, (j + 1) * CL)
            old = raw[slot, 0, j].reshape(CL, HD).astype(jnp.float32)
            new = jnp.dot(put[j], new_pair[h, rows, :], preferred_element_type=jnp.float32)
            old = turn(old, cosine[span, :], sine[span, :])
            keys[span, :] = (old * stay[span, :] + new[:, :HD]).astype(jnp.bfloat16)
            old = raw[slot, 1, j].reshape(CL, HD).astype(jnp.float32)
            vals[span, :] = (old * stay[span, :] + new[:, HD:]).astype(jnp.bfloat16)
        for t in range(CPR):
            later = q[pl.ds(h * CPR + t, CPR - t)].reshape((CPR - t) * block, HD)
            scores[t * block :, t * CL : (t + 1) * CL] = lax.dot_general(
                later,
                keys[t * CL : (t + 1) * CL, :],
                (((1,), (1,)), ((), ())),
                preferred_element_type=jnp.float32,
            )
        for j in range(CPR):
            extent = (j + 1) * CL
            part = scores[j * block : (j + 1) * block, :extent]
            bias = jnp.concatenate([seen[j]] * group, axis=0)
            last = part[:, j * CL :] + bias
            part = last if j == 0 else jnp.concatenate([part[:, : j * CL], last], axis=1)
            row_max = jnp.max(part, axis=1, keepdims=True)
            weights = jnp.exp2((part - row_max) * SCALE_LOG2E)
            row_sum = jnp.sum(weights, axis=1, keepdims=True)
            mixed = jnp.dot(
                weights.astype(jnp.bfloat16),
                vals[:extent, :],
                preferred_element_type=jnp.float32,
            )
            mixed = (mixed / row_sum).astype(jnp.bfloat16)
            for g in range(group):
                start = pl.multiple_of((h * group + g) * HD, HD)
                out[j * RPC : (j + 1) * RPC, pl.ds(start, HD)] = mixed[g * RPC : (g + 1) * RPC]
        return carry

    lax.fori_loop(0, heads_kv, head, 0)


SMEM = pl.BlockSpec(memory_space=pltpu.SMEM)
VMEM = pl.BlockSpec(memory_space=pltpu.VMEM)
ANY = pl.BlockSpec(memory_space=pl.ANY)


def local(span_keys, span_values, span_row, span_lists, recompute_pos, fresh_q, fresh_k, fresh_v):
    n_store = lax.axis_size("store")
    n_req = lax.axis_size("req")
    n_tp = lax.axis_size("tp")
    n_all = n_store * n_req * n_tp
    peers = n_store * n_req
    shard_rows, tok_dev, width = span_keys.shape
    heads_kv = width // HD
    heads_q = fresh_q.shape[2] // HD
    group = heads_q // heads_kv
    bf16 = jnp.bfloat16

    def params(mebibytes):
        return pltpu.CompilerParams(vmem_limit_bytes=mebibytes << 20)


    assert n_req == BLOCKS and shard_rows * n_req == span_row.shape[0]
    plan, place = pl.pallas_call(
        functools.partial(ask_kernel, shard_rows),
        out_shape=(
            jax.ShapeDtypeStruct((peers, LANES), jnp.int32),
            jax.ShapeDtypeStruct((2, CPR), jnp.int32),
        ),
        in_specs=[SMEM, SMEM],
        out_specs=(VMEM, SMEM),
        name="ask",
    )(span_row, span_lists)
    plans = lax.all_to_all(plan, ("store", "req"), split_axis=0, concat_axis=0, tiled=True)
    piece = (2, tok_dev, width)
    climb = [(k, (k + 1) % n_req) for k in range(n_req)]
    sink = [(k, (k - 1) % n_req) for k in range(n_req)]

    def gather(size, plans, span_keys, span_values):
        moves = jax.ShapeDtypeStruct((size, tok_dev, width), bf16)
        move = pl.pallas_call(
            functools.partial(move_kernel, size),
            out_shape=(moves, moves),
            in_specs=[ANY, ANY],
            out_specs=(ANY, ANY),
            scratch_shapes=[
                pltpu.SMEM((peers, LANES), jnp.int32),
                pltpu.VMEM((shard_rows, tok_dev, width), bf16),
                pltpu.VMEM((size + SLOTS, tok_dev, width), bf16),
                pltpu.VMEM((size + SLOTS, tok_dev, width), bf16),
                pltpu.SemaphoreType.DMA((2,)),
            ],
            compiler_params=params(60),
            name="move",
        )
        came = []
        for table in (span_keys, span_values):
            ups, downs = move(plans, table)
            came.append(lax.ppermute(ups, "req", climb))
            came.append(lax.ppermute(downs, "req", sink))
            plans, span_keys, span_values, _ = lax.optimization_barrier(
                (plans, span_keys, span_values, ups)
            )
        own = pl.pallas_call(
            own_kernel,
            out_shape=jax.ShapeDtypeStruct((peers, SLOTS) + piece, bf16),
            in_specs=[SMEM, ANY, ANY],
            out_specs=ANY,
            scratch_shapes=[
                pltpu.VMEM((2, shard_rows, tok_dev, width), bf16),
                pltpu.VMEM((peers, SLOTS) + piece, bf16),
                pltpu.SemaphoreType.DMA((2,)),
                pltpu.SemaphoreType.DMA,
            ],
            compiler_params=params(58),
            name="own",
        )(plans, span_keys, span_values)
        return pl.pallas_call(
            patch_kernel,
            out_shape=jax.ShapeDtypeStruct((peers, SLOTS) + piece, bf16),
            in_specs=[SMEM] + [VMEM] * 4 + [ANY],
            out_specs=ANY,
            scratch_shapes=[pltpu.SemaphoreType.DMA],
            input_output_aliases={5: 0},
            compiler_params=params(40),
            name="patch",
        )(plans, *came, own)

    level = pl.pallas_call(
        level_kernel,
        out_shape=jax.ShapeDtypeStruct((1,), jnp.int32),
        in_specs=[VMEM],
        out_specs=SMEM,
        name="level",
    )(plans)[0]
    most = SLOTS * peers
    send = lax.switch(
        level,
        [functools.partial(gather, size) for size in SIZES + (most,)],
        plans,
        span_keys,
        span_values,
    )
    got = lax.all_to_all(send, ("store", "req"), split_axis=0, concat_axis=0, tiled=True)
    got = got.reshape((n_store, n_req, SLOTS) + piece)

    places, raw_q, raw_k, _ = lax.optimization_barrier((recompute_pos, fresh_q, fresh_k, send))
    places = places[0]
    raw_k = raw_k[0]
    new_v = fresh_v[0]
    angles = places.astype(jnp.float32)[:, None] * jnp.asarray(FREQ)[None, :]
    cosine = jnp.cos(angles)
    sine = jnp.sin(angles)
    queries, new_pair = pl.pallas_call(
        functools.partial(fresh_kernel, heads_kv, group),
        out_shape=(
            jax.ShapeDtypeStruct((heads_kv * CPR, group * RPC, HD), bf16),
            jax.ShapeDtypeStruct((heads_kv, RC, 2 * HD), bf16),
        ),
        in_specs=[VMEM] * 5,
        out_specs=(VMEM, VMEM),
        compiler_params=params(16),
        name="fresh",
    )(
        raw_q[0],
        raw_k,
        new_v,
        jnp.concatenate([cosine, cosine], axis=1),
        jnp.concatenate([-sine, sine], axis=1),
    )
    places_col = places[:, None]
    places_row = places.reshape(CPR, RPC)

    part = pl.pallas_call(
        functools.partial(drift_kernel, span_row.shape[0]),
        out_shape=jax.ShapeDtypeStruct((n_all, LANES), jnp.float32),
        in_specs=[SMEM, SMEM, VMEM, VMEM, VMEM, ANY],
        out_specs=VMEM,
        scratch_shapes=[
            pltpu.VMEM((CPR, n_store, tok_dev, width), bf16),
            pltpu.VMEM((CPR, n_store, tok_dev, width), bf16),
            pltpu.SemaphoreType.DMA((2, CPR)),
        ],
        compiler_params=params(50),
        cost_estimate=pl.CostEstimate(
            flops=4 * RC * CL * width, bytes_accessed=4 * CTX * width, transcendentals=0
        ),
        name="drift",
    )(place, span_lists, places_col, raw_k, new_v, got)
    parts = lax.all_to_all(part, ("store", "req", "tp"), split_axis=0, concat_axis=0, tiled=True)

    attended = pl.pallas_call(
        functools.partial(attend_kernel, heads_kv, group),
        out_shape=jax.ShapeDtypeStruct((RC, heads_q * HD), bf16),
        in_specs=[SMEM] + [VMEM] * 8 + [ANY],
        out_specs=VMEM,
        scratch_shapes=[
            pltpu.VMEM((2, 2, CPR, n_store, tok_dev, HD), bf16),
            pltpu.VMEM((CTX, HD), bf16),
            pltpu.VMEM((CTX, HD), bf16),
            pltpu.VMEM((CPR, RPC, CL), jnp.float32),
            pltpu.VMEM((CPR, CL, RPC), bf16),
            pltpu.VMEM((CTX, HD), jnp.float32),
            pltpu.VMEM((CTX, HD), jnp.float32),
            pltpu.VMEM((CTX, HD), jnp.float32),
            pltpu.VMEM((CPR * group * RPC, CTX), jnp.float32),
            pltpu.SemaphoreType.DMA((2,)),
        ],
        compiler_params=params(50),
        cost_estimate=pl.CostEstimate(
            flops=2 * heads_q * RC * CTX * HD * 2,
            bytes_accessed=4 * CTX * width + 4 * RC * heads_q * HD,
            transcendentals=heads_q * RC * CTX // 2,
        ),
        name="attend",
    )(
        place,
        places_row,
        places_col,
        queries,
        new_pair,
        jnp.asarray(COS_SPAN),
        jnp.asarray(SIN_SPAN),
        jnp.asarray(COS_TOKEN),
        jnp.asarray(SIN_TOKEN),
        got,
    )
    per_dest = span_row.shape[0] // n_all
    drift_part = jnp.sum(parts, axis=0)[:per_dest]
    return (attended[None], drift_part)


def solution(mesh):
    in_specs = (
        P("req", "store", "tp"),
        P("req", "store", "tp"),
        P(),
        P(("store", "req"), None),
        P(("store", "req"), None),
        P(("store", "req"), None, "tp"),
        P(("store", "req"), None, "tp"),
        P(("store", "req"), None, "tp"),
    )
    out_specs = (P(("store", "req"), None, "tp"), P(("store", "req", "tp")))
    return jax.shard_map(local, mesh=mesh, in_specs=in_specs, out_specs=out_specs, check_vma=False)
```

```python
import functools

import jax
import jax.numpy as jnp
import numpy as np
from jax import lax
from jax.experimental import pallas as pl
from jax.experimental.pallas import tpu as pltpu
from jax.sharding import PartitionSpec as P

HD = 128
HALF = HD // 2
CPR = 8
RPC = 16
CL = 256
CTX = CPR * CL
RC = CPR * RPC
KVH = 8
BLOCKS = 4
SLOTS = CPR // BLOCKS
SIZES = (22, 23, 24, 25, 26, 27, 28, 30, 33, 38)
KEPT, UP, DOWN, FROM_BELOW, FROM_ABOVE, LOADS = 0, 4, 8, 12, 13, 16
LANES = 128
SCALE_LOG2E = float(HD ** -0.5 * np.log2(np.e))

FREQ = np.exp(-np.log(500000.0) * np.arange(HALF) / HALF).astype(np.float32)


def angle_tables(positions):
    angles = positions[:, None].astype(np.float64) * FREQ[None, :].astype(np.float64)
    cosine = np.cos(angles).astype(np.float32)
    sine = np.sin(angles).astype(np.float32)
    return (
        np.concatenate([cosine, cosine], axis=1),
        np.concatenate([-sine, sine], axis=1),
    )


COS_SPAN, SIN_SPAN = angle_tables(CL * np.arange(CPR))
COS_TOKEN, SIN_TOKEN = angle_tables(np.arange(CL))


def turn(x, cosine, sine):
    return x * cosine + pltpu.roll(x, HALF, 1) * sine


def ask_kernel(shard_rows, span_row, span_lists, plan, place):
    spans = [span_row[span_lists[0, j]] for j in range(CPR)]
    homes = [row // shard_rows for row in spans]
    rows = [row % shard_rows for row in spans]
    one = [[jnp.where(home == k, 1, 0) for home in homes] for k in range(BLOCKS)]
    counts = [sum(one[k]) for k in range(BLOCKS)]
    sums = []
    total = jnp.int32(0)
    for k in range(BLOCKS):
        total = total + counts[k] - SLOTS
        sums.append(total)
    low, high = jnp.minimum(sums[0], sums[1]), jnp.maximum(sums[0], sums[1])
    low2, high2 = jnp.minimum(sums[2], sums[3]), jnp.maximum(sums[2], sums[3])
    middle, middle2 = jnp.maximum(low, low2), jnp.minimum(high, high2)
    first, second = jnp.minimum(middle, middle2), jnp.maximum(middle, middle2)
    whole = sums[0] + sums[1] + sums[2] + sums[3]
    mixed = lax.rem(sum(span_lists[0, j] for j in range(CPR)), 4) == 0
    level = jnp.abs(whole - BLOCKS * first) <= jnp.abs(whole - BLOCKS * second)
    shift = jnp.where(level != mixed, first, second)
    flow = [x - shift for x in sums]
    up = [jnp.maximum(x, 0) for x in flow]
    down = [jnp.maximum(-flow[k - 1], 0) for k in range(BLOCKS)]
    keep = [counts[k] - up[k] - down[k] for k in range(BLOCKS)]

    block = lax.broadcasted_iota(jnp.int32, plan.shape, 0) % BLOCKS
    lane = lax.broadcasted_iota(jnp.int32, plan.shape, 1)
    out = jnp.zeros(plan.shape, jnp.int32)
    for k in range(BLOCKS):
        own = block == k
        heads = (
            (KEPT, keep[k]),
            (UP, up[k]),
            (DOWN, down[k]),
            (FROM_BELOW, up[k - 1]),
            (FROM_ABOVE, down[(k + 1) % BLOCKS]),
        )
        for at, value in heads:
            out = jnp.where(own & (lane == at), value, out)
        out = jnp.where(lane == LOADS + k, up[k], out)
        out = jnp.where(lane == LOADS + BLOCKS + k, down[k], out)

    def of(table, k):
        value = table[0]
        for i in range(1, BLOCKS):
            value = jnp.where(k == i, table[i], value)
        return value

    base_below = [keep[k] for k in range(BLOCKS)]
    base_above = [keep[k] + up[k - 1] for k in range(BLOCKS)]
    for j in range(CPR):
        home = homes[j]
        rank = jnp.int32(0)
        for i in range(j):
            rank = rank + jnp.where(homes[i] == home, 1, 0)
        kept = of(keep, home)
        after = rank - kept
        ups = of(up, home)
        stays = after < 0
        climbs = after < ups
        at = jnp.where(
            stays, KEPT + 1 + rank, jnp.where(climbs, UP + 1 + after, DOWN + 1 + after - ups)
        )
        out = jnp.where((block == home) & (lane == at), rows[j], out)
        above = lax.rem(home + 1, BLOCKS)
        below = lax.rem(home + BLOCKS - 1, BLOCKS)
        place[0, j] = jnp.where(stays, home, jnp.where(climbs, above, below))
        place[1, j] = jnp.where(
            stays,
            rank,
            jnp.where(climbs, of(base_below, above) + after, of(base_above, below) + after - ups),
        )
    plan[...] = out


def level_kernel(plan, out):
    lane = lax.broadcasted_iota(jnp.int32, (1, LANES), 1)
    loads = jnp.sum(plan[...].astype(jnp.float32), axis=0, keepdims=True)
    loads = jnp.where((lane >= LOADS) & (lane < LOADS + 2 * BLOCKS), loads, 0.0)
    load = jnp.max(loads).astype(jnp.int32)
    level = jnp.int32(0)
    for size in SIZES:
        level = level + jnp.where(load > size, 1, 0)
    out[0] = level


def move_kernel(size, plans, table, up_out, down_out, plan, rows, up_stage, down_stage, sems):
    loads = [
        pltpu.make_async_copy(plans, plan, sems.at[0]),
        pltpu.make_async_copy(table, rows, sems.at[1]),
    ]
    for load in loads:
        load.start()
    for load in loads:
        load.wait()

    def fill(r, marks):
        ends = []
        for at, stage, mark in ((UP, up_stage, marks[0]), (DOWN, down_stage, marks[1])):
            for i in range(SLOTS):
                stage[mark + i] = rows[plan[r, at + 1 + i]]
            ends.append(mark + plan[r, at])
        return tuple(ends)

    lax.fori_loop(0, plan.shape[0], fill, (jnp.int32(0), jnp.int32(0)), unroll=4)
    stores = [
        pltpu.make_async_copy(stage.at[pl.ds(0, size)], out, sems.at[i])
        for i, (stage, out) in enumerate(((up_stage, up_out), (down_stage, down_out)))
    ]
    for store in stores:
        store.start()
    for store in stores:
        store.wait()


def own_kernel(plan, keys, values, send, pool, stage, sems, out_sem):
    loads = [
        pltpu.make_async_copy(table, pool.at[i], sems.at[i])
        for i, table in enumerate((keys, values))
    ]
    for load in loads:
        load.start()
    for load in loads:
        load.wait()

    def fill(r, carry):
        for t in range(SLOTS):
            row = plan[r, KEPT + 1 + t]
            stage[r, t, 0] = pool[0, row]
            stage[r, t, 1] = pool[1, row]
        pltpu.make_async_copy(stage.at[r], send.at[r], out_sem).start()
        return carry

    lax.fori_loop(0, send.shape[0], fill, 0, unroll=4)
    pltpu.make_async_copy(stage, send, out_sem).wait()


def patch_kernel(plan, below_k, above_k, below_v, above_v, own, send, sem):
    def fill(r, marks):
        kept = plan[r, KEPT]
        second = kept + plan[r, FROM_BELOW]
        for t in range(SLOTS):

            @pl.when((t >= kept) & (t < second))
            def _():
                row = marks[0] + t - kept
                pltpu.make_async_copy(below_k.at[row], send.at[r, t, 0], sem).start()
                pltpu.make_async_copy(below_v.at[row], send.at[r, t, 1], sem).start()

            @pl.when(t >= second)
            def _():
                row = marks[1] + t - second
                pltpu.make_async_copy(above_k.at[row], send.at[r, t, 0], sem).start()
                pltpu.make_async_copy(above_v.at[row], send.at[r, t, 1], sem).start()

        return marks[0] + plan[r, FROM_BELOW], marks[1] + plan[r, FROM_ABOVE]

    ends = lax.fori_loop(0, send.shape[0], fill, (jnp.int32(0), jnp.int32(0)), unroll=4)

    def drain(i, carry):
        pltpu.make_async_copy(send.at[0, 0], send.at[0, 0], sem).wait()
        return carry

    lax.fori_loop(0, ends[0] + ends[1], drain, 0)


def fresh_kernel(heads_kv, group, q, k, v, cosine, sine, q_out, pair_out):
    cos = cosine[...]
    sin = sine[...]
    for h in range(heads_kv):
        cols = slice(h * HD, (h + 1) * HD)
        turned = turn(k[:, cols].astype(jnp.float32), cos, sin)
        pair_out[h, :, :HD] = turned.astype(jnp.bfloat16)
        pair_out[h, :, HD:] = v[:, cols]
        for g in range(group):
            n = h * group + g
            turned = turn(q[:, n * HD : (n + 1) * HD].astype(jnp.float32), cos, sin)
            turned = turned.astype(jnp.bfloat16)
            for j in range(CPR):
                q_out[h * CPR + j, g * RPC : (g + 1) * RPC, :] = turned[j * RPC : (j + 1) * RPC]


def drift_kernel(
    total_spans, place, span_lists, places_col, fresh_k, fresh_v, got, drift, kbuf, vbuf, sems
):
    copies = []
    for j in range(CPR):
        for which, buf in enumerate((kbuf, vbuf)):
            copy = pltpu.make_async_copy(
                got.at[:, place[0, j], place[1, j], which], buf.at[j], sems.at[which, j]
            )
            copy.start()
            copies.append(copy)
    width = fresh_k.shape[1]
    dest = lax.broadcasted_iota(jnp.int32, drift.shape, 0)
    lane = lax.broadcasted_iota(jnp.int32, drift.shape, 1)
    per_dest = total_spans // drift.shape[0]
    token = lax.broadcasted_iota(jnp.int32, (RPC, CL), 1)
    total = jnp.zeros(drift.shape, jnp.float32)
    for j in range(CPR):
        rows = slice(j * RPC, (j + 1) * RPC)
        take = (token + j * CL == places_col[rows, :]).astype(jnp.float32)
        take = take.astype(jnp.bfloat16)
        gap = jnp.zeros((RPC, width), jnp.float32)
        copies[2 * j].wait()
        copies[2 * j + 1].wait()
        for buf, fresh in ((kbuf, fresh_k), (vbuf, fresh_v)):
            cached = jnp.dot(take, buf[j].reshape(CL, width), preferred_element_type=jnp.float32)
            delta = fresh[rows, :].astype(jnp.float32) - cached
            gap = gap + delta * delta
        share = jnp.sum(gap) * (1.0 / (2.0 * KVH * HD * RPC))
        chosen = span_lists[0, j]
        total = total + jnp.where(
            (dest == chosen // per_dest) & (lane == chosen % per_dest), share, 0.0
        )
    drift[...] = total


def attend_kernel(
    heads_kv,
    group,
    place,
    places_row,
    places_col,
    q,
    new_pair,
    cos_span,
    sin_span,
    cos_token,
    sin_token,
    got,
    out,
    raw,
    keys,
    vals,
    seen,
    put,
    stay,
    cosine,
    sine,
    scores,
    sems,
):
    def loads(h, slot):
        cols = pl.ds(pl.multiple_of(h * HD, HD), HD)
        return [
            pltpu.make_async_copy(
                got.at[:, place[0, j], place[1, j], which, :, cols],
                raw.at[slot, which, j],
                sems.at[slot],
            )
            for which in range(2)
            for j in range(CPR)
        ]

    for load in loads(0, 0):
        load.start()
    block = group * RPC
    token_lane = lax.broadcasted_iota(jnp.int32, (RPC, CL), 1)
    token_row = lax.broadcasted_iota(jnp.int32, (CL, RPC), 0)
    ones = jnp.ones((RPC, HD), jnp.bfloat16)
    for j in range(CPR):
        rows = slice(j * RPC, (j + 1) * RPC)
        span = slice(j * CL, (j + 1) * CL)
        seen[j] = jnp.where(token_lane + j * CL <= places_col[rows, :], 0.0, -1e30)
        hits = (token_row + j * CL == places_row[j : j + 1, :]).astype(jnp.float32)
        hits = hits.astype(jnp.bfloat16)
        put[j] = hits
        stay[span, :] = 1.0 - jnp.dot(hits, ones, preferred_element_type=jnp.float32)
        ca, sa = cos_span[j : j + 1, :], sin_span[j : j + 1, :]
        cb, sb = cos_token[...], sin_token[...]
        cosine[span, :] = ca * cb - sa * sb
        sine[span, :] = sa * cb + ca * sb

    def head(h, carry):
        slot = lax.rem(h, 2)
        pltpu.make_async_copy(raw.at[slot], raw.at[slot], sems.at[slot]).wait()

        @pl.when(h + 1 < heads_kv)
        def _():
            for load in loads(h + 1, 1 - slot):
                load.start()

        for j in range(CPR):
            rows = slice(j * RPC, (j + 1) * RPC)
            span = slice(j * CL, (j + 1) * CL)
            old = raw[slot, 0, j].reshape(CL, HD).astype(jnp.float32)
            new = jnp.dot(put[j], new_pair[h, rows, :], preferred_element_type=jnp.float32)
            old = turn(old, cosine[span, :], sine[span, :])
            keys[span, :] = (old * stay[span, :] + new[:, :HD]).astype(jnp.bfloat16)
            old = raw[slot, 1, j].reshape(CL, HD).astype(jnp.float32)
            vals[span, :] = (old * stay[span, :] + new[:, HD:]).astype(jnp.bfloat16)
        for t in range(CPR):
            later = q[pl.ds(h * CPR + t, CPR - t)].reshape((CPR - t) * block, HD)
            scores[t * block :, t * CL : (t + 1) * CL] = lax.dot_general(
                later,
                keys[t * CL : (t + 1) * CL, :],
                (((1,), (1,)), ((), ())),
                preferred_element_type=jnp.float32,
            )
        for j in range(CPR):
            extent = (j + 1) * CL
            part = scores[j * block : (j + 1) * block, :extent]
            bias = jnp.concatenate([seen[j]] * group, axis=0)
            last = part[:, j * CL :] + bias
            part = last if j == 0 else jnp.concatenate([part[:, : j * CL], last], axis=1)
            row_max = jnp.max(part, axis=1, keepdims=True)
            weights = jnp.exp2((part - row_max) * SCALE_LOG2E)
            row_sum = jnp.sum(weights, axis=1, keepdims=True)
            mixed = jnp.dot(
                weights.astype(jnp.bfloat16),
                vals[:extent, :],
                preferred_element_type=jnp.float32,
            )
            mixed = (mixed / row_sum).astype(jnp.bfloat16)
            for g in range(group):
                start = pl.multiple_of((h * group + g) * HD, HD)
                out[j * RPC : (j + 1) * RPC, pl.ds(start, HD)] = mixed[g * RPC : (g + 1) * RPC]
        return carry

    lax.fori_loop(0, heads_kv, head, 0)


SMEM = pl.BlockSpec(memory_space=pltpu.SMEM)
VMEM = pl.BlockSpec(memory_space=pltpu.VMEM)
ANY = pl.BlockSpec(memory_space=pl.ANY)


def local(span_keys, span_values, span_row, span_lists, recompute_pos, fresh_q, fresh_k, fresh_v):
    n_store = lax.axis_size("store")
    n_req = lax.axis_size("req")
    n_tp = lax.axis_size("tp")
    n_all = n_store * n_req * n_tp
    peers = n_store * n_req
    shard_rows, tok_dev, width = span_keys.shape
    heads_kv = width // HD
    heads_q = fresh_q.shape[2] // HD
    group = heads_q // heads_kv
    bf16 = jnp.bfloat16

    def params(mebibytes):
        return pltpu.CompilerParams(vmem_limit_bytes=mebibytes << 20)


    assert n_req == BLOCKS and shard_rows * n_req == span_row.shape[0]
    plan, place = pl.pallas_call(
        functools.partial(ask_kernel, shard_rows),
        out_shape=(
            jax.ShapeDtypeStruct((peers, LANES), jnp.int32),
            jax.ShapeDtypeStruct((2, CPR), jnp.int32),
        ),
        in_specs=[SMEM, SMEM],
        out_specs=(VMEM, SMEM),
        name="ask",
    )(span_row, span_lists)
    plans = lax.all_to_all(plan, ("store", "req"), split_axis=0, concat_axis=0, tiled=True)
    piece = (2, tok_dev, width)
    climb = [(k, (k + 1) % n_req) for k in range(n_req)]
    sink = [(k, (k - 1) % n_req) for k in range(n_req)]

    def gather(size, plans, span_keys, span_values):
        moves = jax.ShapeDtypeStruct((size, tok_dev, width), bf16)
        move = pl.pallas_call(
            functools.partial(move_kernel, size),
            out_shape=(moves, moves),
            in_specs=[ANY, ANY],
            out_specs=(ANY, ANY),
            scratch_shapes=[
                pltpu.SMEM((peers, LANES), jnp.int32),
                pltpu.VMEM((shard_rows, tok_dev, width), bf16),
                pltpu.VMEM((size + SLOTS, tok_dev, width), bf16),
                pltpu.VMEM((size + SLOTS, tok_dev, width), bf16),
                pltpu.SemaphoreType.DMA((2,)),
            ],
            compiler_params=params(60),
            name="move",
        )
        came = []
        for table in (span_keys, span_values):
            ups, downs = move(plans, table)
            came.append(lax.ppermute(ups, "req", climb))
            came.append(lax.ppermute(downs, "req", sink))
            plans, span_keys, span_values, _ = lax.optimization_barrier(
                (plans, span_keys, span_values, ups)
            )
        own = pl.pallas_call(
            own_kernel,
            out_shape=jax.ShapeDtypeStruct((peers, SLOTS) + piece, bf16),
            in_specs=[SMEM, ANY, ANY],
            out_specs=ANY,
            scratch_shapes=[
                pltpu.VMEM((2, shard_rows, tok_dev, width), bf16),
                pltpu.VMEM((peers, SLOTS) + piece, bf16),
                pltpu.SemaphoreType.DMA((2,)),
                pltpu.SemaphoreType.DMA,
            ],
            compiler_params=params(58),
            name="own",
        )(plans, span_keys, span_values)
        return pl.pallas_call(
            patch_kernel,
            out_shape=jax.ShapeDtypeStruct((peers, SLOTS) + piece, bf16),
            in_specs=[SMEM] + [VMEM] * 4 + [ANY],
            out_specs=ANY,
            scratch_shapes=[pltpu.SemaphoreType.DMA],
            input_output_aliases={5: 0},
            compiler_params=params(40),
            name="patch",
        )(plans, *came, own)

    level = pl.pallas_call(
        level_kernel,
        out_shape=jax.ShapeDtypeStruct((1,), jnp.int32),
        in_specs=[VMEM],
        out_specs=SMEM,
        name="level",
    )(plans)[0]
    most = SLOTS * peers
    send = lax.switch(
        level,
        [functools.partial(gather, size) for size in SIZES + (most,)],
        plans,
        span_keys,
        span_values,
    )
    got = lax.all_to_all(send, ("store", "req"), split_axis=0, concat_axis=0, tiled=True)
    got = got.reshape((n_store, n_req, SLOTS) + piece)

    places, raw_q, raw_k, _ = lax.optimization_barrier((recompute_pos, fresh_q, fresh_k, send))
    places = places[0]
    raw_k = raw_k[0]
    new_v = fresh_v[0]
    angles = places.astype(jnp.float32)[:, None] * jnp.asarray(FREQ)[None, :]
    cosine = jnp.cos(angles)
    sine = jnp.sin(angles)
    queries, new_pair = pl.pallas_call(
        functools.partial(fresh_kernel, heads_kv, group),
        out_shape=(
            jax.ShapeDtypeStruct((heads_kv * CPR, group * RPC, HD), bf16),
            jax.ShapeDtypeStruct((heads_kv, RC, 2 * HD), bf16),
        ),
        in_specs=[VMEM] * 5,
        out_specs=(VMEM, VMEM),
        compiler_params=params(16),
        name="fresh",
    )(
        raw_q[0],
        raw_k,
        new_v,
        jnp.concatenate([cosine, cosine], axis=1),
        jnp.concatenate([-sine, sine], axis=1),
    )
    places_col = places[:, None]
    places_row = places.reshape(CPR, RPC)

    part = pl.pallas_call(
        functools.partial(drift_kernel, span_row.shape[0]),
        out_shape=jax.ShapeDtypeStruct((n_all, LANES), jnp.float32),
        in_specs=[SMEM, SMEM, VMEM, VMEM, VMEM, ANY],
        out_specs=VMEM,
        scratch_shapes=[
            pltpu.VMEM((CPR, n_store, tok_dev, width), bf16),
            pltpu.VMEM((CPR, n_store, tok_dev, width), bf16),
            pltpu.SemaphoreType.DMA((2, CPR)),
        ],
        compiler_params=params(50),
        cost_estimate=pl.CostEstimate(
            flops=4 * RC * CL * width, bytes_accessed=4 * CTX * width, transcendentals=0
        ),
        name="drift",
    )(place, span_lists, places_col, raw_k, new_v, got)
    parts = lax.all_to_all(part, ("store", "req", "tp"), split_axis=0, concat_axis=0, tiled=True)

    attended = pl.pallas_call(
        functools.partial(attend_kernel, heads_kv, group),
        out_shape=jax.ShapeDtypeStruct((RC, heads_q * HD), bf16),
        in_specs=[SMEM] + [VMEM] * 8 + [ANY],
        out_specs=VMEM,
        scratch_shapes=[
            pltpu.VMEM((2, 2, CPR, n_store, tok_dev, HD), bf16),
            pltpu.VMEM((CTX, HD), bf16),
            pltpu.VMEM((CTX, HD), bf16),
            pltpu.VMEM((CPR, RPC, CL), jnp.float32),
            pltpu.VMEM((CPR, CL, RPC), bf16),
            pltpu.VMEM((CTX, HD), jnp.float32),
            pltpu.VMEM((CTX, HD), jnp.float32),
            pltpu.VMEM((CTX, HD), jnp.float32),
            pltpu.VMEM((CPR * group * RPC, CTX), jnp.float32),
            pltpu.SemaphoreType.DMA((2,)),
        ],
        compiler_params=params(50),
        cost_estimate=pl.CostEstimate(
            flops=2 * heads_q * RC * CTX * HD * 2,
            bytes_accessed=4 * CTX * width + 4 * RC * heads_q * HD,
            transcendentals=heads_q * RC * CTX // 2,
        ),
        name="attend",
    )(
        place,
        places_row,
        places_col,
        queries,
        new_pair,
        jnp.asarray(COS_SPAN),
        jnp.asarray(SIN_SPAN),
        jnp.asarray(COS_TOKEN),
        jnp.asarray(SIN_TOKEN),
        got,
    )
    per_dest = span_row.shape[0] // n_all
    drift_part = jnp.sum(parts, axis=0)[:per_dest]
    return (attended[None], drift_part)


def solution(mesh):
    in_specs = (
        P("req", "store", "tp"),
        P("req", "store", "tp"),
        P(),
        P(("store", "req"), None),
        P(("store", "req"), None),
        P(("store", "req"), None, "tp"),
        P(("store", "req"), None, "tp"),
        P(("store", "req"), None, "tp"),
    )
    out_specs = (P(("store", "req"), None, "tp"), P(("store", "req", "tp")))
    return jax.shard_map(local, mesh=mesh, in_specs=in_specs, out_specs=out_specs, check_vma=False)
```
